128 devices in a mesh: group: 8 (over y, core), rep: 16 (over x, z).
Axes of the slice: x: 4, y: 4, z: 4, core: 2. Of those that a mesh axis runs over, the one named last changes fastest.
Arguments:
- table_hot: bfloat16 [131072, 512], P(('group', 'rep')), may hold values from -6 to 6
- table_mid: bfloat16 [524288, 128], P(('group', 'rep')), may hold values from -6 to 6
- table_cold: bfloat16 [524288, 128], P(('group', 'rep')), may hold values from -6 to 6
- proj_hot: bfloat16 [512, 256], replicated, may hold values from -0.25 to 0.25
- proj_mid: bfloat16 [128, 256], replicated, may hold values from -0.5 to 0.5
- proj_cold: bfloat16 [32, 256], replicated, may hold values from -1 to 1
- tower_in: bfloat16 [256, 1024], replicated, may hold values from -0.375 to 0.375
- tower_out: bfloat16 [1024, 256], replicated, may hold values from -0.1875 to 0.1875
- queries: bfloat16 [65536, 256], P(('group', 'rep')), may hold values from -68 to 68
- labels: int32 [65536], P(('group', 'rep')), may hold values from 0 to 8191
- item_slot: int32 [128, 4, 1024], P(('group', 'rep')), may hold values from 0 to 1023
- item_block: int32 [128, 4, 1024], P(('group', 'rep')), may hold values from 0 to 2
- serve_rows: int32 [128, 3, 1024], P(('group', 'rep')), may hold values from 0 to 16383, as said below
Outputs:
- query_loss: float32 [65536], P(('group', 'rep'))
- query_grad: float32 [65536, 256], P(('group', 'rep'))
- grad_hot: float32 [131072, 512], P(('group', 'rep'))
- grad_mid: float32 [524288, 128], P(('group', 'rep'))
- grad_cold: float32 [524288, 128], P(('group', 'rep'))
- grad_proj_hot: float32 [512, 256], P(None, 'rep')
- grad_proj_mid: float32 [128, 256], P(None, 'rep')
- grad_proj_cold: float32 [32, 256], P(None, 'rep')
- grad_tower_in: float32 [256, 1024], P(None, 'rep')
- grad_tower_out: float32 [1024, 256], P(None, 'rep')
The draws below stay inside these ranges and needn't reach their ends.
Inputs may be any that keep to these rules, and one draw needn't show every extreme that they name: serve_rows[o, b, d * 8 + c] is a row of owner o's shard of block b that requester d sees in slot c; for block 0 it is below 1024, for block 1 below 4096, for block 2 below 16384; the 8 rows that one owner serves to one requester in one block are distinct.
All inputs are finite; a program needn't handle non-finite values.
Results may differ from the reference program's by a relative error of at most 0.02.
The reference program's roundings to bfloat16 on the way count: a program that leaves them out, or rounds other values in their place, can miss the bound.
Values may be sent and summed in bfloat16 or wider, within the bound.
A program may use at most 128 MiB of HBM per device.

```python
import math
import jax
import jax.numpy as jnp
import numpy as np
from jax import lax

D = 256
H = 1024
W_HOT = 512
W_MID = 128
W_COLD = 32
FIELDS = 4
CAP = 8
ITEMS_DEV = 1024
Q_DEV = 512
R_HOT_DEV = 1024
R_MID_DEV = 4096
R_COLD_DEV = 16384
SLOTS = 1024
N_GROUP = 8
N_REP = 16


def draw_queries(key, part):
    full_shape = (N_GROUP * N_REP * Q_DEV, D)
    first_key = jax.random.fold_in(jax.random.fold_in(key, 11), 0)
    return jnp.clip(jax.random.normal(first_key, full_shape, jnp.float32), -4.0, 4.0).astype(jnp.bfloat16)


def draw_serve_rows(key, part):
    devices = N_GROUP * N_REP
    slot_total = devices * CAP
    stride = jnp.array([R_HOT_DEV // CAP, R_MID_DEV // CAP, R_COLD_DEV // CAP], jnp.int32)
    offset = jax.random.randint(jax.random.fold_in(key, 23), (devices, 3, slot_total), 0, 1 << 20) % stride[None, :, None]
    slot_pos = jnp.arange(slot_total, dtype=jnp.int32) % CAP
    return (slot_pos[None, None, :] * stride[None, :, None] + offset).astype(jnp.int32)


def with_ends(values, key, least, largest):
    shape = values.shape
    index_at = [jax.random.randint(jax.random.fold_in(key, axis), (), 0, shape[axis]) for axis in range(len(shape))]
    values = values.at[tuple(index_at)].set(least)
    longest = shape.index(max(shape))
    index_at[longest] = (index_at[longest] + 1) % shape[longest]
    return values.at[tuple(index_at)].set(largest)


def shard_levels(key, dims, cuts, smallest, top_value):
    def one(axis_at, parts):
        draws = jax.random.uniform(jax.random.fold_in(jax.random.fold_in(key, 6), axis_at), (parts,), jnp.float32, smallest / len(cuts), top_value / len(cuts))
        return jnp.repeat(jnp.exp(draws), dims[axis_at] // parts).reshape((-1,) + (1,) * (len(dims) - axis_at - 1))

    factor_of = one(*cuts[0])
    for cut in cuts[1:]:
        factor_of = factor_of * one(*cut)
    return factor_of


def rank_table(count, skew):
    loads = [(1 << 20) // math.isqrt(standing ** skew) + 1 for standing in range(1, count + 1)]
    scale = 1 + sum(loads) // (1 << 30)
    return np.cumsum(np.array([max(1, weight // scale) for weight in loads]))


def ranked(stream_key, extent, number_of, skew):
    table = rank_table(number_of, skew)
    ticket = jax.random.randint(jax.random.fold_in(stream_key, 1), extent, 0, int(table[number_of - 1]))
    standing = jnp.searchsorted(jnp.asarray(table, jnp.int32), ticket, side="right")
    return jax.random.permutation(jax.random.fold_in(stream_key, 2), number_of)[standing].astype(jnp.int32)


def scatter_about(rng, dims, scale, reach, cuts=(), kind=jnp.bfloat16):
    drawn = jax.random.normal(rng, dims, jnp.float32) * scale
    if len(cuts) > 0:
        drawn = shard_levels(rng, dims, cuts, -0.22, 0.18) * drawn
    return jnp.clip(drawn, min=-reach, max=reach).astype(kind)


def setup_inputs(seed: int = 0) -> dict:
    seeds = jax.random.split(jax.random.key(seed), 14)
    table_hot = scatter_about(seeds[0], (N_GROUP * N_REP * R_HOT_DEV, W_HOT), 1.0, 6.0, ((0, 128),))
    table_mid = scatter_about(seeds[1], (N_GROUP * N_REP * R_MID_DEV, W_MID), 1.0, 6.0, ((0, 128),))
    table_cold = scatter_about(seeds[2], (N_GROUP * N_REP * R_COLD_DEV // 4, 4 * W_COLD), 1.0, 6.0, ((0, 128),))
    proj_hot = scatter_about(seeds[3], (W_HOT, D), W_HOT ** -0.5, 0.25)
    proj_mid = scatter_about(seeds[4], (W_MID, D), W_MID ** -0.5, 0.5)
    proj_cold = scatter_about(seeds[5], (W_COLD, D), W_COLD ** -0.5, 1.0)
    tower_in = scatter_about(seeds[6], (D, H), D ** -0.5, 0.375)
    tower_out = scatter_about(seeds[7], (H, D), H ** -0.5, 0.1875)
    queries = draw_queries(jax.random.fold_in(seeds[13], 71), 0)
    labels = with_ends(jax.random.randint(seeds[9], (N_GROUP * N_REP * Q_DEV,), 0, N_GROUP * ITEMS_DEV), jax.random.fold_in(seeds[9], 1), 0, (N_GROUP * ITEMS_DEV) - 1).astype(jnp.int32)
    item_slot = with_ends(ranked(seeds[10], (N_GROUP * N_REP, FIELDS, ITEMS_DEV), SLOTS, 1), jax.random.fold_in(seeds[10], 3), 0, SLOTS - 1).astype(jnp.int32)
    item_block = with_ends(jax.random.randint(seeds[11], (N_GROUP * N_REP, FIELDS, ITEMS_DEV), 0, 3), jax.random.fold_in(seeds[11], 1), 0, 2).astype(jnp.int32)
    serve_rows = draw_serve_rows(jax.random.fold_in(seeds[13], 71), 0)
    return {"table_hot": table_hot, "table_mid": table_mid, "table_cold": table_cold, "proj_hot": proj_hot, "proj_mid": proj_mid, "proj_cold": proj_cold, "tower_in": tower_in, "tower_out": tower_out, "queries": queries, "labels": labels, "item_slot": item_slot, "item_block": item_block, "serve_rows": serve_rows}


NORM_EPS = 1e-06
LOGIT_SCALE = 0.2

def silu_slope(pre_act):
    sigmoid = jax.nn.sigmoid(pre_act)
    return sigmoid * (1.0 + pre_act * (1.0 - sigmoid))

def pick_cold(cold_lines, row_ids, col_width):
    pieces = cold_lines.reshape(cold_lines.shape[0], 4, col_width)
    select = jnp.arange(4, dtype=jnp.int32)[None, :] == (row_ids % 4).astype(jnp.int32)[:, None]
    return lax.optimization_barrier(jnp.sum(jnp.where(select[:, :, None], pieces, jnp.zeros((), pieces.dtype)), axis=1)).astype(pieces.dtype)

def cold_add(row_ids, values):
    select = (jnp.arange(4, dtype=jnp.int32)[None, :] == (row_ids % 4).astype(jnp.int32)[:, None]).astype(jnp.float32)
    spread = (select[:, :, None] * values[:, None, :]).reshape(row_ids.shape[0], 4 * W_COLD)
    return jnp.zeros((R_COLD_DEV // 4, 4 * W_COLD), jnp.float32).at[(row_ids // 4).astype(jnp.int32)].add(spread)

def contract(left_rows, right_rows):
    return lax.dot_general(left_rows, right_rows, (((0,), (0,)), ((), ())), preferred_element_type=jnp.float32)

def unproject(slot_grad, weight):
    return lax.dot_general(slot_grad, weight, (((1,), (1,)), ((), ())), preferred_element_type=jnp.float32)

def reference(table_hot, table_mid, table_cold, proj_hot, proj_mid, proj_cold, tower_in, tower_out, queries, labels, item_slot, item_block, serve_rows):
    devices = N_GROUP * N_REP
    slot_total = devices * CAP
    hot_shards = table_hot.reshape(devices, R_HOT_DEV, W_HOT)
    mid_shards = table_mid.reshape(devices, R_MID_DEV, W_MID)
    cold_shards = table_cold.reshape(devices, R_COLD_DEV // 4, 4 * W_COLD)
    owner_hot = jax.vmap(lambda shard_table, row_ids: shard_table[row_ids])(hot_shards, serve_rows[:, 0])
    owner_mid = jax.vmap(lambda shard_table, row_ids: shard_table[row_ids])(mid_shards, serve_rows[:, 1])
    owner_cold = jax.vmap(lambda shard_table, row_ids: pick_cold(shard_table[row_ids // 4], row_ids, W_COLD))(cold_shards, serve_rows[:, 2])

    def to_requester(owned):
        col_width = owned.shape[-1]
        return owned.reshape(devices, devices, CAP, col_width).transpose(1, 0, 2, 3).reshape(devices * slot_total, col_width)
    raw_hot = to_requester(owner_hot)
    raw_mid = to_requester(owner_mid)
    raw_cold = to_requester(owner_cold)

    def project(raw_rows, weight):
        return jnp.dot(raw_rows, weight, preferred_element_type=jnp.float32).astype(jnp.bfloat16).reshape(devices, slot_total, D)
    slot_table = jnp.concatenate([project(raw_hot, proj_hot), project(raw_mid, proj_mid), project(raw_cold, proj_cold)], axis=1)
    slot_index = (item_block * slot_total + item_slot).astype(jnp.int32)
    gathered = jax.vmap(lambda table_rows, which: table_rows[which])(slot_table, slot_index)
    pooled = lax.optimization_barrier(jnp.sum(gathered.astype(jnp.float32), axis=1)).astype(jnp.bfloat16).reshape(devices * ITEMS_DEV, D)
    pre_act = jnp.dot(pooled, tower_in, preferred_element_type=jnp.float32)
    hidden = jax.nn.silu(pre_act).astype(jnp.bfloat16)
    residual = pooled.astype(jnp.float32) + jnp.dot(hidden, tower_out, preferred_element_type=jnp.float32)
    inv_rms = lax.rsqrt(lax.optimization_barrier(jnp.mean(residual * residual, axis=1, keepdims=True)) + NORM_EPS)
    vectors = (residual * inv_rms).astype(jnp.bfloat16)
    negatives = vectors.reshape(N_GROUP, N_REP, ITEMS_DEV, D).transpose(1, 0, 2, 3).reshape(N_REP, N_GROUP * ITEMS_DEV, D)
    group_queries = queries.reshape(N_GROUP, N_REP, Q_DEV, D).transpose(1, 0, 2, 3).reshape(N_REP, N_GROUP * Q_DEV, D)
    group_labels = labels.reshape(N_GROUP, N_REP, Q_DEV).transpose(1, 0, 2).reshape(N_REP, N_GROUP * Q_DEV)

    def one_group(group_args):
        negs_here, queries_here, labels_here = group_args
        scores = lax.dot_general(queries_here, negs_here, (((1,), (1,)), ((), ())), preferred_element_type=jnp.float32) * LOGIT_SCALE
        row_max = lax.optimization_barrier(jnp.max(scores, axis=1, keepdims=True))
        log_total = row_max[:, 0] + jnp.log(lax.optimization_barrier(jnp.sum(jnp.exp(scores - row_max), axis=1)))
        onehot = jnp.arange(scores.shape[1], dtype=jnp.int32)[None, :] == labels_here[:, None]
        picked = lax.optimization_barrier(jnp.sum(jnp.where(onehot, scores, jnp.zeros((), jnp.float32)), axis=1))
        score_grad = (jnp.exp(scores - log_total[:, None]) - onehot.astype(jnp.float32)).astype(jnp.bfloat16)
        query_grad = LOGIT_SCALE * jnp.dot(score_grad, negs_here, preferred_element_type=jnp.float32)
        neg_grad = LOGIT_SCALE * contract(score_grad, queries_here)
        return (log_total - picked, query_grad, neg_grad)
    loss_all, qgrad_all, neg_grad = lax.map(one_group, (negatives, group_queries, group_labels))
    query_loss = loss_all.reshape(N_REP, N_GROUP, Q_DEV).transpose(1, 0, 2).reshape(-1)
    query_grad = qgrad_all.reshape(N_REP, N_GROUP, Q_DEV, D).transpose(1, 0, 2, 3).reshape(-1, D)
    vec_grad = neg_grad.reshape(N_REP, N_GROUP, ITEMS_DEV, D).transpose(1, 0, 2, 3).reshape(-1, D)
    dot_wide = lax.optimization_barrier(jnp.sum(vec_grad * residual, axis=1, keepdims=True))
    wide_grad = inv_rms * vec_grad - inv_rms ** 3 / D * residual * dot_wide
    wide_low = wide_grad.astype(jnp.bfloat16)
    hidden_grad = unproject(wide_low, tower_out)
    pre_grad = (hidden_grad * silu_slope(pre_act)).astype(jnp.bfloat16)
    pooled_grad = (unproject(pre_grad, tower_in) + wide_grad).astype(jnp.bfloat16).reshape(devices, ITEMS_DEV, D)

    def slot_sum(item_grad, which):
        stacked = jnp.broadcast_to(item_grad.astype(jnp.float32)[None], (FIELDS, ITEMS_DEV, D)).reshape(-1, D)
        return jax.ops.segment_sum(stacked, which.reshape(-1), num_segments=3 * slot_total)
    slot_grad = jax.vmap(slot_sum)(pooled_grad, slot_index).astype(jnp.bfloat16)
    grad_hot_slots = slot_grad[:, :slot_total].reshape(-1, D)
    grad_mid_slots = slot_grad[:, slot_total:2 * slot_total].reshape(-1, D)
    grad_cold_slots = slot_grad[:, 2 * slot_total:].reshape(-1, D)

    def to_owner(values):
        col_width = values.shape[-1]
        return values.reshape(devices, devices, CAP, col_width).transpose(1, 0, 2, 3).reshape(devices, slot_total, col_width)
    back_hot = to_owner(unproject(grad_hot_slots, proj_hot))
    back_mid = to_owner(unproject(grad_mid_slots, proj_mid))
    back_cold = to_owner(unproject(grad_cold_slots, proj_cold))
    grad_hot = jax.vmap(lambda row_ids, values: jnp.zeros((R_HOT_DEV, W_HOT), jnp.float32).at[row_ids].add(values))(serve_rows[:, 0], back_hot).reshape(-1, W_HOT)
    grad_mid = jax.vmap(lambda row_ids, values: jnp.zeros((R_MID_DEV, W_MID), jnp.float32).at[row_ids].add(values))(serve_rows[:, 1], back_mid).reshape(-1, W_MID)
    grad_cold = jax.vmap(cold_add)(serve_rows[:, 2], back_cold).reshape(-1, 4 * W_COLD)
    grad_proj_hot = contract(raw_hot, grad_hot_slots)
    grad_proj_mid = contract(raw_mid, grad_mid_slots)
    grad_proj_cold = contract(raw_cold, grad_cold_slots)
    grad_tower_in = contract(pooled, pre_grad)
    grad_tower_out = contract(hidden, wide_low)
    return (query_loss, query_grad, grad_hot, grad_mid, grad_cold, grad_proj_hot, grad_proj_mid, grad_proj_cold, grad_tower_in, grad_tower_out)
```

```python
import functools

import jax
import jax.numpy as jnp
from jax import lax
from jax.experimental import pallas as pl
from jax.experimental.pallas import tpu as pltpu
from jax.sharding import PartitionSpec as P

NORM_EPS = 1e-06
LOGIT_SCALE = 0.2
BF = jnp.bfloat16
F32 = jnp.float32
BOTH = ("group", "rep")


def mm(a, b):
    return lax.dot_general(a, b, (((1,), (0,)), ((), ())), preferred_element_type=F32)


def mm_nt(a, b):
    return lax.dot_general(a, b, (((1,), (1,)), ((), ())), preferred_element_type=F32)


def mm_tn(a, b):
    return lax.dot_general(a, b, (((0,), (0,)), ((), ())), preferred_element_type=F32)


def chosen(index, count):
    return (index[:, None] == lax.broadcasted_iota(jnp.int32, (1, count), 1)).astype(BF)


def silu_slope(pre_act):
    sigmoid = jax.nn.sigmoid(pre_act)
    return sigmoid * (1.0 + pre_act * (1.0 - sigmoid))


def stats_kernel(vec_ref, q_ref, lab_ref, lse_ref, pick_ref):
    st = mm_nt(vec_ref[...], q_ref[...]) * LOGIT_SCALE
    top = jnp.max(st, axis=0, keepdims=True)
    total = jnp.sum(jnp.exp(st - top), axis=0, keepdims=True)
    lse_ref[...] = top + jnp.log(total)
    rows = lax.broadcasted_iota(jnp.int32, st.shape, 0)
    pick_ref[...] = jnp.sum(jnp.where(rows == lab_ref[...], st, 0.0), axis=0, keepdims=True)


def grads_kernel(vec_ref, vec_t_ref, q_ref, lab_ref, lse_ref, vg_ref, qg_ref, tot_ref):
    @pl.when(pl.program_id(0) == 0)
    def _():
        vg_ref[...] = jnp.zeros_like(vg_ref)

    lses = lse_ref[...]
    top = jnp.max(lses, axis=0, keepdims=True)
    tot = top + jnp.log(jnp.sum(jnp.exp(lses - top), axis=0, keepdims=True))
    tot_ref[...] = tot
    st = mm_nt(vec_ref[...], q_ref[...]) * LOGIT_SCALE
    rows = lax.broadcasted_iota(jnp.int32, st.shape, 0)
    grad = (jnp.exp(st - tot) - jnp.where(rows == lab_ref[...], 1.0, 0.0)).astype(BF)
    vg_ref[...] += mm(grad, q_ref[...])
    qg_ref[0] = (LOGIT_SCALE * mm(vec_t_ref[...], grad)).astype(BF)


def local(
    table_hot,
    table_mid,
    table_cold,
    proj_hot,
    proj_mid,
    proj_cold,
    tower_in,
    tower_out,
    queries,
    labels,
    item_slot,
    item_block,
    serve_rows,
):
    group_count = lax.axis_size("group")
    rep_count = lax.axis_size("rep")
    devices = group_count * rep_count
    group_at = lax.axis_index("group")
    slots = serve_rows.shape[2]
    each = slots // devices
    width = tower_in.shape[0]
    hidden_width = tower_in.shape[1]
    items = item_slot.shape[2]
    fields = item_slot.shape[1]
    q_each = queries.shape[0]
    q_all = q_each * group_count
    cold_w = proj_cold.shape[0]
    packs = 128 // cold_w
    packed = slots // packs
    served = serve_rows[0]
    lanes = lax.broadcasted_iota(jnp.int32, (1, 128), 1)
    lane_seg = lanes // cold_w
    fold = (
        lax.broadcasted_iota(jnp.int32, (128, 128), 0) % cold_w
        == lax.broadcasted_iota(jnp.int32, (128, 128), 1) % cold_w
    ).astype(BF)
    slot_ids = lax.broadcasted_iota(jnp.int32, (slots, 1), 0)
    in_pack = (slot_ids % packs) == lane_seg
    in_line = (served[2] % packs)[:, None] == lane_seg
    pick_hot = chosen(served[0], table_hot.shape[0])
    pick_mid = chosen(served[1], table_mid.shape[0])
    pick_line = chosen(served[2] // packs, table_cold.shape[0])
    group_of = (
        lax.broadcasted_iota(jnp.int32, (packed, 1), 0)
        == lax.broadcasted_iota(jnp.int32, (1, slots), 1) // packs
    ).astype(BF)

    q_group = lax.all_gather(queries, "group", axis=0, tiled=True)
    lab_group = lax.all_gather(labels, "group", axis=0, tiled=True)

    rows_hot = mm(pick_hot, table_hot).astype(BF)
    near_hot = mm(rows_hot, proj_hot).astype(BF)
    rows_mid = mm(pick_mid, table_mid).astype(BF)
    lines = mm(pick_line, table_cold).astype(BF)
    zero = jnp.zeros((), BF)
    spread = mm(jnp.where(in_line, lines, zero), fold).astype(BF)
    rows_cold = mm(group_of, jnp.where(in_pack, spread, zero)).astype(BF)
    send = jnp.concatenate(
        [
            near_hot[:, :128].reshape(devices, each, 128),
            near_hot[:, 128:].reshape(devices, each, 128),
            rows_mid.reshape(devices, each, 128),
            rows_cold.reshape(devices, each // packs, 128),
        ],
        axis=1,
    )
    got = lax.all_to_all(send, BOTH, split_axis=0, concat_axis=0, tiled=True)
    hot = jnp.concatenate([got[:, :each], got[:, each : 2 * each]], axis=2).reshape(slots, width)
    raw_mid = got[:, 2 * each : 3 * each].reshape(slots, 128)
    raw_cold = got[:, 3 * each :].reshape(packed, 128)
    near_mid = mm(raw_mid, proj_mid).astype(BF)
    near_cold = [
        mm(raw_cold[:, s * cold_w : (s + 1) * cold_w], proj_cold).astype(BF) for s in range(packs)
    ]
    slot_table = jnp.concatenate([hot, near_mid, *near_cold], axis=0)
    slot = item_slot[0]
    block = item_block[0]
    slot = jnp.where(block == 2, (slot % packs) * packed + slot // packs, slot)
    where = block * slots + slot
    use = functools.reduce(
        jnp.add, [chosen(where[f], 3 * slots) for f in range(fields)]
    )
    pooled = mm(use, slot_table).astype(BF)
    pre_act = mm(pooled, tower_in)
    hidden = jax.nn.silu(pre_act).astype(BF)
    residual = pooled.astype(F32) + mm(hidden, tower_out)
    inv_rms = lax.rsqrt(jnp.mean(residual * residual, axis=1, keepdims=True) + NORM_EPS)
    vectors = (residual * inv_rms).astype(BF)

    lab_local = (lab_group - group_at * items).reshape(1, q_all)
    full = lambda shape: pl.BlockSpec(shape, lambda i: (0, 0))
    row = lambda n: pl.BlockSpec((n, q_each), lambda i: (0, i))
    params = pltpu.CompilerParams(dimension_semantics=("arbitrary",), vmem_limit_bytes=40 << 20)
    lse, pick = pl.pallas_call(
        stats_kernel,
        grid=(group_count,),
        in_specs=[full((items, width)), pl.BlockSpec((q_each, width), lambda i: (i, 0)), row(1)],
        out_specs=[row(1), row(1)],
        out_shape=[jax.ShapeDtypeStruct((1, q_all), F32)] * 2,
        compiler_params=params,
    )(vectors, q_group, lab_local)
    both = lax.all_gather(jnp.concatenate([lse, pick], axis=0), "group", axis=0, tiled=False)
    lses = both[:, 0]
    my_pick = jnp.sum(
        lax.dynamic_slice(both, (0, 1, group_at * q_each), (group_count, 1, q_each))[:, 0], axis=0
    )
    vec_grad, qg_parts, tot = pl.pallas_call(
        grads_kernel,
        grid=(group_count,),
        in_specs=[
            full((items, width)),
            full((width, items)),
            pl.BlockSpec((q_each, width), lambda i: (i, 0)),
            row(1),
            row(group_count),
        ],
        out_specs=[
            full((items, width)),
            pl.BlockSpec((1, width, q_each), lambda i: (i, 0, 0)),
            row(1),
        ],
        out_shape=[
            jax.ShapeDtypeStruct((items, width), F32),
            jax.ShapeDtypeStruct((group_count, width, q_each), BF),
            jax.ShapeDtypeStruct((1, q_all), F32),
        ],
        compiler_params=params,
    )(vectors, vectors.T, q_group, lab_local, lses)
    vec_grad = LOGIT_SCALE * vec_grad
    qg_got = lax.all_to_all(qg_parts, "group", split_axis=0, concat_axis=0, tiled=True)
    query_grad = jnp.sum(qg_got.astype(F32), axis=0).T
    query_loss = lax.dynamic_slice(tot, (0, group_at * q_each), (1, q_each))[0] - my_pick

    dot_wide = jnp.sum(vec_grad * residual, axis=1, keepdims=True)
    wide_grad = inv_rms * vec_grad - inv_rms**3 / width * residual * dot_wide
    wide_low = wide_grad.astype(BF)
    pre_grad = (mm_nt(wide_low, tower_out) * silu_slope(pre_act)).astype(BF)
    pooled_grad = (mm_nt(pre_grad, tower_in) + wide_grad).astype(BF)
    slot_grad = mm_tn(use, pooled_grad).astype(BF)
    sg_hot = slot_grad[:slots]
    sg_mid = slot_grad[slots : 2 * slots]
    sg_cold = [
        slot_grad[2 * slots + s * packed : 2 * slots + (s + 1) * packed] for s in range(packs)
    ]
    back_mid = mm_nt(sg_mid, proj_mid).astype(BF)
    back_cold = jnp.concatenate([mm_nt(g, proj_cold).astype(BF) for g in sg_cold], axis=1)
    send_back = jnp.concatenate(
        [
            sg_hot[:, :128].reshape(devices, each, 128),
            sg_hot[:, 128:].reshape(devices, each, 128),
            back_mid.reshape(devices, each, 128),
            back_cold.reshape(devices, each // packs, 128),
        ],
        axis=1,
    )
    back = lax.all_to_all(send_back, BOTH, split_axis=0, concat_axis=0, tiled=True)
    own_hot = jnp.concatenate([back[:, :each], back[:, each : 2 * each]], axis=2)
    own_hot = own_hot.reshape(slots, width)
    own_mid = back[:, 2 * each : 3 * each].reshape(slots, 128)
    own_cold = back[:, 3 * each :].reshape(packed, 128)
    grad_hot = mm_tn(pick_hot, mm_nt(own_hot, proj_hot).astype(BF))
    grad_mid = mm_tn(pick_mid, own_mid)
    opened = mm_tn(group_of, own_cold).astype(BF)
    opened = mm(jnp.where(in_pack, opened, zero), fold).astype(BF)
    grad_cold = mm_tn(pick_line, jnp.where(in_line, opened, zero))

    def by_rep(total):
        blocks = total.reshape(rep_count, total.shape[0] // rep_count, total.shape[1])
        wide = max(total.shape[1], 128)
        blocks = jnp.pad(blocks, ((0, 0), (0, 0), (0, wide - total.shape[1])))
        return [blocks[:, :, k : k + 128] for k in range(0, wide, 128)]

    in_t = mm_tn(pre_grad, pooled)
    out_t = mm_tn(wide_low, hidden)
    ph_t = mm_tn(own_hot, rows_hot)
    pm_t = mm_tn(sg_mid, raw_mid)
    pc_t = functools.reduce(
        jnp.add,
        [
            mm_tn(sg_cold[s], raw_cold[:, s * cold_w : (s + 1) * cold_w])
            for s in range(packs)
        ],
    )
    parts = [by_rep(t) for t in (in_t, out_t, ph_t, pm_t, pc_t)]
    stack = jnp.concatenate([p for group in parts for p in group], axis=1)
    mine = lax.psum_scatter(stack, "rep", scatter_dimension=0, tiled=True)[0]
    mine = lax.psum(mine, "group")
    outs, at = [], 0
    for group, t in zip(parts, (in_t, out_t, ph_t, pm_t, pc_t)):
        cols = []
        for p in group:
            cols.append(mine[at : at + p.shape[1]])
            at += p.shape[1]
        outs.append(jnp.concatenate(cols, axis=1)[:, : t.shape[1]].T)
    g_in, g_out, g_ph, g_pm, g_pc = outs
    return (
        query_loss,
        query_grad,
        grad_hot,
        grad_mid,
        grad_cold,
        g_ph,
        g_pm,
        g_pc,
        g_in,
        g_out,
    )


def solution(mesh):
    split = P(BOTH)
    return jax.shard_map(
        local,
        mesh=mesh,
        in_specs=(split,) * 3 + (P(),) * 5 + (split,) * 5,
        out_specs=(split,) * 5 + (P(None, "rep"),) * 5,
        check_vma=False,
    )
```

```python
import functools

import jax
import jax.numpy as jnp
from jax import lax
from jax.experimental import pallas as pl
from jax.experimental.pallas import tpu as pltpu
from jax.sharding import PartitionSpec as P

NORM_EPS = 1e-06
LOGIT_SCALE = 0.2
BF = jnp.bfloat16
F32 = jnp.float32
BOTH = ("group", "rep")
MESH = pl.DeviceIdType.MESH
SCALE2 = LOGIT_SCALE * 1.4426950408889634
LN2 = 0.6931471805599453
DMA = pltpu.SemaphoreType.DMA


def mm(a, b):
    return lax.dot_general(a, b, (((1,), (0,)), ((), ())), preferred_element_type=F32)


def mm_nt(a, b):
    return lax.dot_general(a, b, (((1,), (1,)), ((), ())), preferred_element_type=F32)


def mm_tn(a, b):
    return lax.dot_general(a, b, (((0,), (0,)), ((), ())), preferred_element_type=F32)


def flat(block):
    lead = block.shape[0] * block.shape[1]
    return block.astype(F32).reshape(lead, block.shape[2]).astype(BF)


def tiled(value):
    return value.reshape(value.shape[0] // 8, 8, value.shape[1])


def picks(index, shape, axis):
    return jnp.where(index == lax.broadcasted_iota(jnp.int32, shape, axis), 1.0, 0.0)


def step_kernel(
    t_hot, t_mid, t_cold, p_hot, p_mid, p_cold, w_in, w_out, queries, labels, cols, rows,
    back_ref, rows_hot, qg_out, loss_out, fin_ref,
    v_hot, v_mid, v_cold, v_ph, v_in, v_out, q_all, lab_all, send, got, use, use_t, slot_tab,
    raw_mid, raw_cold, pooled, pooled_t, pre, hidden, resid, vec, vec_t, stat, loss_all, vg,
    q_send, q_part, q_sum, q_recv, pre_g, pool_g, wide, low_t, sg_t, back_send, rs_send,
    rs_got, ph_send, ph_got, ph_acc, fin,
    in_sem, f_s, f_r, q_s, q_r, l_s, l_r, st_s, st_r, qp_s, qp_r, qy_s, qy_r, b_s, b_r,
    w_s, w_r, h_s, h_r, a_s, a_r,
):
    g = lax.axis_index("group")
    r = lax.axis_index("rep")
    me = g * 16 + r
    y, c = g // 2, g % 2
    mate = y * 2 + 1 - c

    def peer(k):
        m = (k * 37) % 128
        pg = ((y + (m // 2) % 4) % 4) * 2 + (c + m % 2) % 2
        pr = ((r // 4 + (m // 8) % 4) % 4) * 4 + (r % 4 + m // 32) % 4
        return pg, pr

    def ship(src, dst, s_sem, r_sem, pg, pr):
        return pltpu.make_async_remote_copy(
            src_ref=src,
            dst_ref=dst,
            send_sem=s_sem,
            recv_sem=r_sem,
            device_id=(pg, pr),
            device_id_type=MESH,
        )

    def loads():
        pairs = (
            (t_hot, v_hot), (p_hot, v_ph), (t_mid, v_mid), (t_cold, v_cold),
            (queries, q_all.at[g]), (w_in, v_in), (w_out, v_out),
        )
        return [pltpu.make_async_copy(a, b, in_sem.at[n]) for n, (a, b) in enumerate(pairs)]

    for copy in loads():
        copy.start()
    barrier = pltpu.get_barrier_semaphore()

    def greet(k, carry):
        pl.semaphore_signal(barrier, inc=1, device_id=peer(k), device_id_type=MESH)
        return carry

    lax.fori_loop(1, 128, greet, 0)
    lab_all[g] = labels[...]
    held = loads()
    for n in range(4):
        held[n].wait()

    lane_seg = lax.broadcasted_iota(jnp.int32, (1, 128), 1) // 32

    def send_rows(k):
        gg = (g + 1 + k) % 8

        def one(j, carry):
            rd = (r + j) % 16
            to = gg * 16 + rd

            @pl.when(to != me)
            def _():
                ship(send.at[to], got.at[me], f_s, f_r, gg, rd).start()

            return carry

        lax.fori_loop(0, 16, one, 0)

    def serve(k, carry):
        gg = (g + 1 + k) % 8
        at = pl.multiple_of(gg * 128, 128)
        idx = cols[pl.ds(at, 128), :]
        hot = mm(picks(idx[:, 0:1], (128, 1024), 1).astype(BF), v_hot[...]).astype(BF)
        rows_hot[pl.ds(at, 128), :] = hot
        near = mm(hot, v_ph[...])
        mid = mm(picks(idx[:, 1:2], (128, 4096), 1).astype(BF), v_mid[...])
        line = mm(picks(idx[:, 2:3] // 4, (128, 4096), 1).astype(BF), v_cold[...])
        line = jnp.where(idx[:, 2:3] % 4 == lane_seg, line, 0.0)
        for n, part in enumerate((near[:, :128], near[:, 128:], mid, line)):
            send[pl.ds(gg * 16, 16), n] = tiled(part).astype(BF)

        @pl.when(k == 1)
        def _():
            pl.semaphore_wait(barrier, 127)

        @pl.when(k > 0)
        def _():
            send_rows(k - 1)

        return carry

    lax.fori_loop(0, 8, serve, 0)
    send_rows(7)
    got[me] = send[me]
    held[4].wait()
    for k in range(1, 4):
        ship(q_all.at[g], q_all.at[g], q_s, q_r.at[0], ((y + k) % 4) * 2 + c, r).start()
    ship(q_all.at[g], q_all.at[g], q_s, q_r.at[1], mate, r).start()
    for k in range(1, 8):
        ship(lab_all.at[g], lab_all.at[g], l_s, l_r, (g + k) % 8, r).start()

    def count_items(i, carry):
        at = pl.multiple_of(i * 128, 128)
        idx = cols[pl.ds(at, 128), :]
        total = picks(idx[:, 4:5], (128, 3072), 1)
        for f in range(5, 8):
            total += picks(idx[:, f : f + 1], (128, 3072), 1)
        use[pl.ds(at, 128), :] = total.astype(BF)
        return carry

    lax.fori_loop(0, 8, count_items, 0)

    def count_slots(i, carry):
        at = pl.multiple_of(i * 256, 256)
        idx = rows[...] - at
        total = picks(idx[0:1], (256, 1024), 0)
        for f in range(1, 4):
            total += picks(idx[f : f + 1], (256, 1024), 0)
        use_t[pl.ds(at, 256), :] = total.astype(BF)
        return carry

    lax.fori_loop(0, 12, count_slots, 0)
    ship(q_all.at[pl.ds(0, 3)], q_all.at[pl.ds(0, 3)], q_s, q_r.at[0], g, r).wait_recv()
    for k in range(1, 4):
        from_y = ((y + k) % 4) * 2 + c
        ship(q_all.at[from_y], q_all.at[from_y], q_s, q_r.at[2], mate, r).start()

    ship(send.at[pl.ds(0, 127)], got.at[pl.ds(0, 127)], f_s, f_r, g, r).wait_recv()

    def fill(i, carry):
        at = pl.multiple_of(i * 256, 256)
        slab = pl.ds(i * 32, 32)
        slot_tab[pl.ds(at, 256), 0:128] = flat(got[slab, 0])
        slot_tab[pl.ds(at, 256), 128:256] = flat(got[slab, 1])
        mid = flat(got[slab, 2])
        raw_mid[pl.ds(at, 256), :] = mid
        slot_tab[pl.ds(1024 + at, 256), :] = mm(mid, p_mid[...]).astype(BF)
        cold = flat(got[slab, 3])
        raw_cold[pl.ds(at, 256), :] = cold
        slot_tab[pl.ds(2048 + at, 256), :] = mm(cold, p_cold[...]).astype(BF)
        return carry

    lax.fori_loop(0, 4, fill, 0)
    held[5].wait()
    held[6].wait()

    def forward(i, carry):
        at = pl.multiple_of(i * 256, 256)
        here = pl.ds(at, 256)
        pool = mm(use[here, :], slot_tab[...])
        low = pool.astype(BF)
        pooled[here, :] = low
        low32 = low.astype(F32)
        pooled_t[:, here] = low32.T.astype(BF)
        u = mm(low, v_in[...])
        pre[here, :] = u
        h = (u * (1.0 / (1.0 + jnp.exp(-u)))).astype(BF)
        hidden[here, :] = h
        res = low32 + mm(h, v_out[...])
        resid[here, :] = res
        inv = lax.rsqrt(jnp.mean(res * res, axis=1, keepdims=True) + NORM_EPS)
        v = res * inv
        vec[here, :] = v.astype(BF)
        vec_t[:, here] = v.T.astype(BF)
        return carry

    lax.fori_loop(0, 4, forward, 0)

    ship(q_all.at[g], q_all.at[g], q_s, q_r.at[1], mate, r).wait_recv()
    ship(q_all.at[pl.ds(0, 3)], q_all.at[pl.ds(0, 3)], q_s, q_r.at[2], g, r).wait_recv()
    ship(lab_all.at[pl.ds(0, 7)], lab_all.at[pl.ds(0, 7)], l_s, l_r, g, r).wait_recv()

    def order(t):
        return (t % 4) * 2 + t // 4

    def send_stat(b):
        for k in range(1, 8):
            ship(stat.at[b, g], stat.at[b, g], st_s, st_r.at[b], (g + k) % 8, r).start()

    def label_rows(b):
        return lab_all[b] - g * 1024

    def stats(t, carry):
        b = order(t)
        st = mm_nt(vec[...], q_all[b])
        top = jnp.max(st, axis=0, keepdims=True)
        total = jnp.sum(jnp.exp2(st * SCALE2 - top * SCALE2), axis=0, keepdims=True)
        hit = label_rows(b) == lax.broadcasted_iota(jnp.int32, st.shape, 0)
        stat[b, g, pl.ds(0, 1), :] = top * LOGIT_SCALE + jnp.log(total)
        picked = jnp.sum(jnp.where(hit, st, 0.0), axis=0, keepdims=True)
        stat[b, g, pl.ds(1, 1), :] = picked * LOGIT_SCALE

        @pl.when(t > 0)
        def _():
            send_stat(order(t - 1))

        return carry

    lax.fori_loop(0, 8, stats, 0)
    send_stat(7)
    vg[...] = jnp.zeros_like(vg)

    def grads(b):
        ship(stat.at[b, pl.ds(0, 7)], stat.at[b, pl.ds(0, 7)], st_s, st_r.at[b], g, r).wait_recv()
        lses = [stat[b, n, pl.ds(0, 1), :] for n in range(8)]
        top = functools.reduce(jnp.maximum, lses)
        total = functools.reduce(jnp.add, [jnp.exp(v - top) for v in lses])
        joint = top + jnp.log(total)
        hits = functools.reduce(jnp.add, [stat[b, n, pl.ds(1, 1), :] for n in range(8)])
        loss_all[b] = joint - hits
        st = mm_nt(vec[...], q_all[b])
        hit = label_rows(b) == lax.broadcasted_iota(jnp.int32, st.shape, 0)
        prob = jnp.exp2((st * LOGIT_SCALE - joint) * 1.4426950408889634)
        grad = (prob - jnp.where(hit, 1.0, 0.0)).astype(BF)
        vg[...] += mm(grad, q_all[b])
        return LOGIT_SCALE * mm(vec_t[...], grad)

    def for_mate(i, carry):
        q_send[i] = grads(((y + 1 + i) % 4) * 2 + 1 - c).astype(BF)
        ship(q_send.at[i], q_part.at[i], qp_s, qp_r.at[i], mate, r).start()
        return carry

    lax.fori_loop(0, 4, for_mate, 0)

    def for_self(i, carry):
        at_y = (y + 1 + i) % 4
        mine = grads(at_y * 2 + c)
        ship(q_send.at[i], q_part.at[i], qp_s, qp_r.at[i], mate, r).wait_recv()
        q_sum[i] = (mine + q_part[i].astype(F32)).astype(BF)

        @pl.when(i < 3)
        def _():
            ship(q_sum.at[i], q_recv.at[i], qy_s, qy_r, at_y * 2 + c, r).start()

        return carry

    lax.fori_loop(0, 4, for_self, 0)
    loss_out[...] = loss_all[g]

    def backward(i, carry):
        at = pl.multiple_of(i * 256, 256)
        here = pl.ds(at, 256)
        res = resid[here, :]
        inv = lax.rsqrt(jnp.mean(res * res, axis=1, keepdims=True) + NORM_EPS)
        grad = LOGIT_SCALE * vg[here, :]
        dot_wide = jnp.sum(grad * res, axis=1, keepdims=True)
        wg = inv * grad - (inv * inv * inv / 256.0) * res * dot_wide
        low = wg.astype(BF)
        low_t[:, here] = wg.T.astype(BF)
        u = pre[here, :]
        s = 1.0 / (1.0 + jnp.exp(-u))
        pg = (mm_nt(low, v_out[...]) * (s * (1.0 + u * (1.0 - s)))).astype(BF)
        pre_g[here, :] = pg
        pool_g[here, :] = (mm_nt(pg, v_in[...]) + wg).astype(BF)
        return carry

    lax.fori_loop(0, 4, backward, 0)

    def send_back(t):
        cc = (t + y) % 4

        def one(j, carry):
            to = cc * 32 + (j + r + 16 * c) % 32

            @pl.when(to != me)
            def _():
                ship(back_send.at[to], back_ref.at[me], b_s, b_r, to // 16, to % 16).start()

            return carry

        lax.fori_loop(0, 32, one, 0)

    def slots(t, carry):
        cc = (t + y) % 4
        at = pl.multiple_of(cc * 256, 256)
        slab = pl.ds(cc * 32, 32)
        hot = mm(use_t[pl.ds(at, 256), :], pool_g[...])
        mid = mm(use_t[pl.ds(1024 + at, 256), :], pool_g[...])
        cold = mm(use_t[pl.ds(2048 + at, 256), :], pool_g[...])
        sg_t[:, pl.ds(at, 256)] = mid.T.astype(BF)
        sg_t[:, pl.ds(1024 + at, 256)] = cold.T.astype(BF)
        b_mid = mm_nt(mid.astype(BF), p_mid[...])
        b_cold = mm_nt(cold.astype(BF), p_cold[...])
        for n, part in enumerate((hot[:, :128], hot[:, 128:], b_mid, b_cold)):
            back_send[slab, n] = tiled(part).astype(BF)

        @pl.when(t > 0)
        def _():
            send_back(t - 1)

        return carry

    lax.fori_loop(0, 4, slots, 0)
    send_back(3)
    back_ref[me] = back_send[me]

    def weights(i, carry):
        at = pl.multiple_of(i * 256, 256)
        first = mm(pooled_t[...], pre_g[:, pl.ds(at, 256)]).T
        for n in range(2):
            part = first[:, 128 * n : 128 * n + 128].reshape(4, 8, 8, 128)
            rs_send[pl.ds(i * 4, 4), :, n] = part.astype(BF)
        second = mm(low_t[...], hidden[:, pl.ds(at, 256)])
        for n in range(2):
            part = second[:, 128 * n : 128 * n + 128].reshape(16, 2, 8, 128).astype(BF)
            rs_send[:, i * 2 + n, 2] = part[:, 0]
            rs_send[:, i * 2 + n, 3] = part[:, 1]
        return carry

    lax.fori_loop(0, 4, weights, 0)
    small = [
        mm(sg_t[:, :1024], raw_mid[...]).reshape(16, 2, 8, 128).astype(BF),
        mm(sg_t[:, 1024:], raw_cold[...]).reshape(16, 2, 8, 128).astype(BF),
    ]
    for n in range(8):
        rs_send[:, n, 4] = small[(n // 2) % 2][:, n % 2]

    def send_blocks(k, carry):
        pg, pr = peer(k)
        ship(rs_send.at[pr, pg], rs_got.at[me], w_s, w_r, pg, pr).start()
        return carry

    lax.fori_loop(1, 128, send_blocks, 0)
    rs_got[me] = rs_send[r, g]
    ship(back_send.at[pl.ds(0, 127)], back_ref.at[pl.ds(0, 127)], b_s, b_r, g, r).wait_recv()
    ph_acc[...] = jnp.zeros_like(ph_acc)

    def hot_weights(i, carry):
        slab = pl.ds(i * 32, 32)
        left = back_ref[slab, 0].astype(F32).reshape(256, 128).T.astype(BF)
        right = back_ref[slab, 1].astype(F32).reshape(256, 128).T.astype(BF)
        own = rows_hot[pl.ds(pl.multiple_of(i * 256, 256), 256), :]
        ph_acc[0:128, :] += mm(left, own)
        ph_acc[128:256, :] += mm(right, own)
        return carry

    lax.fori_loop(0, 4, hot_weights, 0)
    for n in range(4):
        part = ph_acc[:, 128 * n : 128 * n + 128].reshape(16, 2, 8, 128).astype(BF)
        ph_send[:, 2 * n] = part[:, 0]
        ph_send[:, 2 * n + 1] = part[:, 1]

    def send_hot(k, carry):
        pg, pr = peer(k)
        ship(ph_send.at[pr, pg], ph_got.at[me], h_s, h_r, pg, pr).start()
        return carry

    lax.fori_loop(1, 128, send_hot, 0)
    ph_got[me] = ph_send[r, g]

    ship(q_sum.at[pl.ds(0, 3)], q_recv, qy_s, qy_r, g, r).wait_recv()
    qg = q_sum[3].astype(F32)
    for n in range(3):
        qg += q_recv[n].astype(F32)
    qg_out[...] = qg

    ship(rs_got.at[pl.ds(0, 127)], rs_got.at[pl.ds(0, 127)], w_s, w_r, g, r).wait_recv()

    def add(k, total):
        return total + rs_got[k].astype(F32)

    fin[g, pl.ds(0, 5)] = lax.fori_loop(0, 128, add, jnp.zeros((5, 8, 128), F32))
    ship(ph_got.at[pl.ds(0, 127)], ph_got.at[pl.ds(0, 127)], h_s, h_r, g, r).wait_recv()

    def add_hot(k, total):
        return total + ph_got[k].astype(F32)

    fin[g, 5] = lax.fori_loop(0, 128, add_hot, jnp.zeros((8, 128), F32))
    for k in range(1, 8):
        ship(fin.at[g], fin.at[g], a_s, a_r, (g + k) % 8, r).start()
    ship(fin.at[pl.ds(0, 7)], fin.at[pl.ds(0, 7)], a_s, a_r, g, r).wait()
    fin_ref[...] = fin[...]

    ship(send.at[pl.ds(0, 127)], got.at[pl.ds(0, 127)], f_s, f_r, g, r).wait_send()
    ship(q_all.at[pl.ds(0, 7)], q_all.at[pl.ds(0, 7)], q_s, q_r.at[0], g, r).wait_send()
    ship(lab_all.at[pl.ds(0, 7)], lab_all.at[pl.ds(0, 7)], l_s, l_r, g, r).wait_send()
    for b in range(8):
        ship(stat.at[b, pl.ds(0, 7)], stat.at[b, pl.ds(0, 7)], st_s, st_r.at[0], g, r).wait_send()
    ship(q_send, q_part, qp_s, qp_r.at[0], g, r).wait_send()
    ship(q_sum.at[pl.ds(0, 3)], q_recv, qy_s, qy_r, g, r).wait_send()
    ship(back_send.at[pl.ds(0, 127)], back_ref.at[pl.ds(0, 127)], b_s, b_r, g, r).wait_send()
    ship(rs_got.at[pl.ds(0, 127)], rs_got.at[pl.ds(0, 127)], w_s, w_r, g, r).wait_send()
    ship(ph_got.at[pl.ds(0, 127)], ph_got.at[pl.ds(0, 127)], h_s, h_r, g, r).wait_send()


def scatter_kernel(back, served, segs, p_hot, out_hot, out_mid, out_cold, b_hot, b_mid, b_cold):
    step = pl.program_id(0)

    @pl.when(step == 0)
    def _():
        lane_seg = lax.broadcasted_iota(jnp.int32, (1, 128), 1) // 32
        for i in range(4):
            here = pl.ds(i * 256, 256)
            slab = pl.ds(i * 32, 32)
            b_hot[here, :] = (
                mm_nt(flat(back[slab, 0]), p_hot[:, 0:128])
                + mm_nt(flat(back[slab, 1]), p_hot[:, 128:256])
            ).astype(BF)
            b_mid[here, :] = flat(back[slab, 2])
            cold = flat(back[slab, 3])
            b_cold[here, :] = jnp.where(segs[here, 3:4] == lane_seg, cold, jnp.zeros((), BF))

    idx = served[...]
    hot = picks(idx[0:1] - step * 128, (128, 1024), 0).astype(BF)
    out_hot[...] = mm(hot, b_hot[...])
    mid = picks(idx[1:2] - step * 512, (512, 1024), 0).astype(BF)
    out_mid[...] = mm(mid, b_mid[...])
    cold = picks(idx[2:3] - step * 512, (512, 1024), 0).astype(BF)
    out_cold[...] = mm(cold, b_cold[...])


def local(
    table_hot,
    table_mid,
    table_cold,
    proj_hot,
    proj_mid,
    proj_cold,
    tower_in,
    tower_out,
    queries,
    labels,
    item_slot,
    item_block,
    serve_rows,
):
    served = serve_rows[0]
    where = item_block[0] * 1024 + item_slot[0]
    segs = served[2:3] % 4
    cols = jnp.concatenate([served, segs, where], axis=0).T
    idx_rows = jnp.concatenate([served[0:2], served[2:3] // 4, segs], axis=0)
    pc4 = jnp.concatenate([proj_cold] * 4, axis=0)
    anywhere = pl.BlockSpec(memory_space=pl.ANY)
    vmem = pl.BlockSpec(memory_space=pltpu.VMEM)
    sds = jax.ShapeDtypeStruct
    V = pltpu.VMEM
    back, _, qg_t, loss, fin = pl.pallas_call(
        step_kernel,
        out_shape=[
            sds((128, 4, 8, 128), BF),
            sds((1024, 512), BF),
            sds((256, 512), F32),
            sds((1, 512), F32),
            sds((8, 6, 8, 128), F32),
        ],
        in_specs=[anywhere] * 4 + [vmem] * 2 + [anywhere] * 3 + [vmem] * 3,
        out_specs=[vmem] * 5,
        scratch_shapes=[
            V((1024, 512), BF), V((4096, 128), BF), V((4096, 128), BF), V((512, 256), BF),
            V((256, 1024), BF), V((1024, 256), BF), V((8, 512, 256), BF), V((8, 1, 512), jnp.int32),
            V((128, 4, 8, 128), BF), V((128, 4, 8, 128), BF), V((1024, 3072), BF),
            V((3072, 1024), BF), V((3072, 256), BF), V((1024, 128), BF), V((1024, 128), BF),
            V((1024, 256), BF), V((256, 1024), BF), V((1024, 1024), F32), V((1024, 1024), BF),
            V((1024, 256), F32), V((1024, 256), BF), V((256, 1024), BF), V((8, 8, 2, 512), F32),
            V((8, 1, 512), F32), V((1024, 256), F32), V((4, 256, 512), BF), V((4, 256, 512), BF),
            V((4, 256, 512), BF), V((3, 256, 512), BF), V((1024, 1024), BF), V((1024, 256), BF),
            V((8, 128), F32), V((256, 1024), BF), V((256, 2048), BF), V((128, 4, 8, 128), BF),
            V((16, 8, 5, 8, 128), BF), V((128, 5, 8, 128), BF), V((16, 8, 8, 128), BF),
            V((128, 8, 128), BF), V((256, 512), F32), V((8, 6, 8, 128), F32),
            DMA((7,)), DMA, DMA, DMA, DMA((3,)), DMA, DMA, DMA, DMA((8,)), DMA, DMA((4,)),
            DMA, DMA, DMA, DMA, DMA, DMA, DMA, DMA, DMA, DMA,
        ],
        compiler_params=pltpu.CompilerParams(
            collective_id=1, has_side_effects=True, vmem_limit_bytes=63 << 20
        ),
        name="step",
    )(
        table_hot, table_mid, table_cold, proj_hot, proj_mid, pc4, tower_in, tower_out, queries,
        labels.reshape(1, 512), cols, where,
    )
    full = lambda a: pl.BlockSpec(a.shape, lambda i: (0,) * a.ndim)
    grad_hot, grad_mid, grad_cold = pl.pallas_call(
        scatter_kernel,
        grid=(8,),
        in_specs=[full(back), full(idx_rows), full(cols), full(proj_hot)],
        out_specs=[
            pl.BlockSpec((128, 512), lambda i: (i, 0)),
            pl.BlockSpec((512, 128), lambda i: (i, 0)),
            pl.BlockSpec((512, 128), lambda i: (i, 0)),
        ],
        out_shape=[sds((1024, 512), F32), sds((4096, 128), F32), sds((4096, 128), F32)],
        scratch_shapes=[V((1024, 512), BF), V((1024, 128), BF), V((1024, 128), BF)],
        compiler_params=pltpu.CompilerParams(
            dimension_semantics=("arbitrary",), vmem_limit_bytes=40 << 20
        ),
        name="scatter",
    )(back, idx_rows, cols, proj_hot)
    g_in = fin[:, 0:2].transpose(1, 3, 0, 2).reshape(256, 64)
    g_out = fin[:, 2:4].transpose(0, 3, 1, 2).reshape(1024, 16)
    pmc = fin[0:4, 4].reshape(2, 2, 8, 128).transpose(0, 3, 1, 2).reshape(2, 128, 16)
    g_pm = pmc[0]
    g_pc = pmc[1].reshape(4, 32, 16).sum(axis=0)
    g_ph = fin[:, 5].reshape(4, 2, 8, 128).transpose(0, 3, 1, 2).reshape(512, 16)
    return (
        loss[0],
        qg_t.T,
        grad_hot,
        grad_mid,
        grad_cold,
        g_ph,
        g_pm,
        g_pc,
        g_in,
        g_out,
    )


def solution(mesh):
    split = P(BOTH)
    return jax.shard_map(
        local,
        mesh=mesh,
        in_specs=(split,) * 3 + (P(),) * 5 + (split,) * 5,
        out_specs=(split,) * 5 + (P(None, "rep"),) * 5,
        check_vma=False,
    )
```

```python
import functools

import jax
import jax.numpy as jnp
from jax import lax
from jax.experimental import pallas as pl
from jax.experimental.pallas import tpu as pltpu
from jax.sharding import PartitionSpec as P

NORM_EPS = 1e-06
LOGIT_SCALE = 0.2
BF = jnp.bfloat16
F32 = jnp.float32
BOTH = ("group", "rep")
MESH = pl.DeviceIdType.MESH
SCALE2 = LOGIT_SCALE * 1.4426950408889634
LN2 = 0.6931471805599453
DMA = pltpu.SemaphoreType.DMA


def mm(a, b):
    return lax.dot_general(a, b, (((1,), (0,)), ((), ())), preferred_element_type=F32)


def mm_nt(a, b):
    return lax.dot_general(a, b, (((1,), (1,)), ((), ())), preferred_element_type=F32)


def mm_tn(a, b):
    return lax.dot_general(a, b, (((0,), (0,)), ((), ())), preferred_element_type=F32)


def flat(block):
    lead = block.shape[0] * block.shape[1]
    return block.astype(F32).reshape(lead, block.shape[2]).astype(BF)


def tiled(value):
    return value.reshape(value.shape[0] // 8, 8, value.shape[1])


def to_col(row):
    return jnp.broadcast_to(row.astype(F32), (128, row.shape[1])).T[:, 0:1].astype(jnp.int32)


def picks(index, shape, axis):
    return jnp.where(index == lax.broadcasted_iota(jnp.int32, shape, axis), 1.0, 0.0)


def step_kernel(
    t_hot, t_mid, t_cold, p_hot, p_mid, proj_cold, w_in, w_out, queries, labels, served,
    item_slot, item_block,
    back_ref, rows_hot, qg_out, loss_out, fin_ref,
    v_hot, v_mid, v_cold, v_ph, v_in, v_out, q_all, lab_all, send, got, use_t, slot_t,
    raw_mid, raw_cold, p_cold, p_mid_t, p_cold_t, pooled_t, pre, hidden, resid, vec, vec_t, stat, loss_all, vg,
    q_send, q_part, q_sum, q_recv, pre_g, pool_g, low_t, sg_t, back_send, rs_part,
    rs_pair, rs_send, rs_got, ph_send, ph_got, ph_acc, fin,
    in_sem, f_s, f_r, q_s, q_r, l_s, l_r, st_s, st_r, qp_s, qp_r, qy_s, qy_r, b_s, b_r,
    wp_s, wp_r, w_s, w_r, h_s, h_r, a_s, a_r,
):
    g = lax.axis_index("group")
    r = lax.axis_index("rep")
    me = g * 16 + r
    y, c = g // 2, g % 2
    mate = y * 2 + 1 - c

    def all_peers(visit, step=1):
        for k in range(0, 8, step):
            pg = lax.rem(g + k, 8)

            def one(j, carry, pg=pg):
                visit(pg, lax.rem(r + j, 16))
                return carry

            lax.fori_loop(0 if k else 1, 16, one, 0)

    def ship(src, dst, s_sem, r_sem, pg, pr):
        return pltpu.make_async_remote_copy(
            src_ref=src,
            dst_ref=dst,
            send_sem=s_sem,
            recv_sem=r_sem,
            device_id=(pg, pr),
            device_id_type=MESH,
        )

    def loads():
        pairs = (
            (t_hot, v_hot), (p_hot, v_ph),
            (t_mid.at[pl.ds(0, 2048)], v_mid.at[:, pl.ds(0, 128)]),
            (t_mid.at[pl.ds(2048, 2048)], v_mid.at[:, pl.ds(128, 128)]),
            (t_cold.at[pl.ds(0, 2048)], v_cold.at[:, pl.ds(0, 128)]),
            (t_cold.at[pl.ds(2048, 2048)], v_cold.at[:, pl.ds(128, 128)]),
            (queries, q_all.at[g]), (w_in, v_in), (w_out, v_out),
        )
        return [pltpu.make_async_copy(a, b, in_sem.at[n]) for n, (a, b) in enumerate(pairs)]

    for copy in loads():
        copy.start()
    barrier = pltpu.get_barrier_semaphore()

    def greet(pg, pr):
        pl.semaphore_signal(barrier, inc=1, device_id=(pg, pr), device_id_type=MESH)

    all_peers(greet)
    lab_all[g] = labels[...]
    held = loads()
    for n in range(4):
        p_cold[pl.ds(32 * n, 32), :] = proj_cold[...]
    p_mid_t[...] = p_mid[...].astype(F32).T.astype(BF)
    p_cold_t[...] = p_cold[...].astype(F32).T.astype(BF)
    for n in range(6):
        held[n].wait()

    lane_seg = lax.broadcasted_iota(jnp.int32, (1, 128), 1) // 32

    def send_rows(k):
        gg = (g + 1 + k) % 8

        def one(j, carry):
            rd = (r + j) % 16
            to = gg * 16 + rd

            @pl.when(to != me)
            def _():
                ship(send.at[to], got.at[me], f_s, f_r, gg, rd).start()

            return carry

        lax.fori_loop(0, 16, one, 0)

    def halves(index, table):
        both = mm(picks(index % 2048, (128, 2048), 1).astype(BF), table[...])
        return jnp.where(index >= 2048, both[:, 128:], both[:, :128])

    def serve(k, carry):
        gg = (g + 1 + k) % 8
        at = pl.multiple_of(gg * 128, 128)
        here = pl.ds(at, 128)
        i_hot, i_mid, i_cold = [to_col(served[pl.ds(n, 1), here]) for n in range(3)]
        hot = mm(picks(i_hot, (128, 1024), 1).astype(BF), v_hot[...]).astype(BF)
        rows_hot[here, :] = hot
        near = mm(hot, v_ph[...])
        mid = halves(i_mid, v_mid)
        line = halves(i_cold // 4, v_cold)
        line = jnp.where(i_cold % 4 == lane_seg, line, 0.0)
        for n, part in enumerate((near[:, :128], near[:, 128:], mid, line)):
            send[pl.ds(gg * 16, 16), n] = tiled(part).astype(BF)
        return carry

    lax.fori_loop(0, 8, serve, 0)
    pl.semaphore_wait(barrier, 127)
    for k in range(8):
        send_rows(k)
    got[me] = send[me]
    held[6].wait()
    for k in range(1, 4):
        ship(q_all.at[g], q_all.at[g], q_s, q_r.at[0], ((y + k) % 4) * 2 + c, r).start()
    ship(q_all.at[g], q_all.at[g], q_s, q_r.at[1], mate, r).start()
    for k in range(1, 8):
        ship(lab_all.at[g], lab_all.at[g], l_s, l_r, (g + k) % 8, r).start()

    where = item_block[...] * 1024 + item_slot[...]

    def count_slots(i, carry):
        at = pl.multiple_of(i * 256, 256)
        idx = where - at
        total = picks(idx[0:1], (256, 1024), 0)
        for f in range(1, 4):
            total += picks(idx[f : f + 1], (256, 1024), 0)
        use_t[pl.ds(at, 256), :] = total.astype(BF)
        return carry

    lax.fori_loop(0, 12, count_slots, 0)
    ship(q_all.at[pl.ds(0, 3)], q_all.at[pl.ds(0, 3)], q_s, q_r.at[0], g, r).wait_recv()
    for k in range(1, 4):
        from_y = ((y + k) % 4) * 2 + c
        ship(q_all.at[from_y], q_all.at[from_y], q_s, q_r.at[2], mate, r).start()

    ship(send.at[pl.ds(0, 127)], got.at[pl.ds(0, 127)], f_s, f_r, g, r).wait_recv()

    def fill(i, carry):
        at = pl.multiple_of(i * 256, 256)
        slab = pl.ds(i * 32, 32)
        for n in range(2):
            near = got[slab, n].astype(F32).reshape(256, 128).T.astype(BF)
            slot_t[pl.ds(128 * n, 128), pl.ds(at, 256)] = near
        mid = flat(got[slab, 2])
        raw_mid[pl.ds(at, 256), :] = mid
        slot_t[:, pl.ds(1024 + at, 256)] = mm_nt(p_mid_t[...], mid).astype(BF)
        cold = flat(got[slab, 3])
        raw_cold[pl.ds(at, 256), :] = cold
        slot_t[:, pl.ds(2048 + at, 256)] = mm_nt(p_cold_t[...], cold).astype(BF)
        return carry

    lax.fori_loop(0, 4, fill, 0)
    held[7].wait()
    held[8].wait()

    def forward(i, carry):
        at = pl.multiple_of(i * 256, 256)
        here = pl.ds(at, 256)
        turned = mm(slot_t[...], use_t[:, here]).astype(BF)
        pooled_t[:, here] = turned
        low32 = turned.astype(F32).T
        low = low32.astype(BF)
        u = mm(low, v_in[...])
        pre[here, :] = u
        h = (u * (1.0 / (1.0 + jnp.exp(-u)))).astype(BF)
        hidden[here, :] = h
        res = low32 + mm(h, v_out[...])
        resid[here, :] = res
        inv = lax.rsqrt(jnp.mean(res * res, axis=1, keepdims=True) + NORM_EPS)
        v = res * inv
        vec[here, :] = v.astype(BF)
        vec_t[:, here] = v.T.astype(BF)
        return carry

    lax.fori_loop(0, 4, forward, 0)

    ship(q_all.at[g], q_all.at[g], q_s, q_r.at[1], mate, r).wait_recv()
    ship(q_all.at[pl.ds(0, 3)], q_all.at[pl.ds(0, 3)], q_s, q_r.at[2], g, r).wait_recv()
    ship(lab_all.at[pl.ds(0, 7)], lab_all.at[pl.ds(0, 7)], l_s, l_r, g, r).wait_recv()

    def order(t):
        return (t % 4) * 2 + t // 4

    def send_stat(b):
        for k in range(1, 8):
            ship(stat.at[b, g], stat.at[b, g], st_s, st_r.at[b], (g + k) % 8, r).start()

    def label_rows(b):
        return lab_all[b] - g * 1024

    def stats(t, carry):
        b = order(t)
        st = mm_nt(vec[...], q_all[b])
        top = jnp.max(st, axis=0, keepdims=True)
        total = jnp.sum(jnp.exp2(st * SCALE2 - top * SCALE2), axis=0, keepdims=True)
        hit = label_rows(b) == lax.broadcasted_iota(jnp.int32, st.shape, 0)
        stat[b, g, pl.ds(0, 1), :] = top * LOGIT_SCALE + jnp.log(total)
        picked = jnp.sum(jnp.where(hit, st, 0.0), axis=0, keepdims=True)
        stat[b, g, pl.ds(1, 1), :] = picked * LOGIT_SCALE

        @pl.when(t > 0)
        def _():
            send_stat(order(t - 1))

        return carry

    lax.fori_loop(0, 8, stats, 0)
    send_stat(7)
    vg[...] = jnp.zeros_like(vg)

    def grads(b):
        ship(stat.at[b, pl.ds(0, 7)], stat.at[b, pl.ds(0, 7)], st_s, st_r.at[b], g, r).wait_recv()
        lses = [stat[b, n, pl.ds(0, 1), :] for n in range(8)]
        top = functools.reduce(jnp.maximum, lses)
        total = functools.reduce(jnp.add, [jnp.exp(v - top) for v in lses])
        joint = top + jnp.log(total)
        hits = functools.reduce(jnp.add, [stat[b, n, pl.ds(1, 1), :] for n in range(8)])
        loss_all[b] = joint - hits
        st = mm_nt(vec[...], q_all[b])
        hit = label_rows(b) == lax.broadcasted_iota(jnp.int32, st.shape, 0)
        prob = jnp.exp2((st * LOGIT_SCALE - joint) * 1.4426950408889634)
        grad = (prob - jnp.where(hit, 1.0, 0.0)).astype(BF)
        vg[...] += mm(grad, q_all[b])
        return LOGIT_SCALE * mm(vec_t[...], grad)

    def for_mate(i, carry):
        q_send[i] = grads(((y + 1 + i) % 4) * 2 + 1 - c).astype(BF)
        ship(q_send.at[i], q_part.at[i], qp_s, qp_r.at[i], mate, r).start()
        return carry

    lax.fori_loop(0, 4, for_mate, 0)

    def for_self(i, carry):
        at_y = (y + 1 + i) % 4
        mine = grads(at_y * 2 + c)
        ship(q_send.at[i], q_part.at[i], qp_s, qp_r.at[i], mate, r).wait_recv()
        q_sum[i] = (mine + q_part[i].astype(F32)).astype(BF)

        @pl.when(i < 3)
        def _():
            ship(q_sum.at[i], q_recv.at[i], qy_s, qy_r, at_y * 2 + c, r).start()

        return carry

    lax.fori_loop(0, 4, for_self, 0)
    loss_out[...] = loss_all[g]

    def backward(i, carry):
        at = pl.multiple_of(i * 256, 256)
        here = pl.ds(at, 256)
        res = resid[here, :]
        inv = lax.rsqrt(jnp.mean(res * res, axis=1, keepdims=True) + NORM_EPS)
        grad = LOGIT_SCALE * vg[here, :]
        dot_wide = jnp.sum(grad * res, axis=1, keepdims=True)
        wg = inv * grad - (inv * inv * inv / 256.0) * res * dot_wide
        low = wg.astype(BF)
        low_t[:, here] = wg.T.astype(BF)
        u = pre[here, :]
        s = 1.0 / (1.0 + jnp.exp(-u))
        pg = (mm_nt(low, v_out[...]) * (s * (1.0 + u * (1.0 - s)))).astype(BF)
        pre_g[here, :] = pg
        pool_g[here, :] = (mm_nt(pg, v_in[...]) + wg).astype(BF)
        return carry

    lax.fori_loop(0, 4, backward, 0)

    def send_back(t):
        cc = (t + y) % 4

        def one(j, carry):
            to = cc * 32 + (j + r + 16 * c) % 32

            @pl.when(to != me)
            def _():
                ship(back_send.at[to], back_ref.at[me], b_s, b_r, to // 16, to % 16).start()

            return carry

        lax.fori_loop(0, 32, one, 0)

    def slots(t, carry):
        cc = (t + y) % 4
        at = pl.multiple_of(cc * 256, 256)
        slab = pl.ds(cc * 32, 32)
        hot = mm(use_t[pl.ds(at, 256), :], pool_g[...])
        mid = mm(use_t[pl.ds(1024 + at, 256), :], pool_g[...])
        cold = mm(use_t[pl.ds(2048 + at, 256), :], pool_g[...])
        sg_t[:, pl.ds(at, 256)] = mid.T.astype(BF)
        sg_t[:, pl.ds(1024 + at, 256)] = cold.T.astype(BF)
        b_mid = mm_nt(mid.astype(BF), p_mid[...])
        b_cold = mm_nt(cold.astype(BF), p_cold[...])
        for n, part in enumerate((hot[:, :128], hot[:, 128:], b_mid, b_cold)):
            back_send[slab, n] = tiled(part).astype(BF)

        @pl.when(t > 0)
        def _():
            send_back(t - 1)

        return carry

    lax.fori_loop(0, 4, slots, 0)
    send_back(3)
    back_ref[me] = back_send[me]

    def weights(i, carry):
        at = pl.multiple_of(i * 256, 256)
        first = mm(pooled_t[...], pre_g[:, pl.ds(at, 256)]).T
        for n in range(2):
            part = first[:, 128 * n : 128 * n + 128].reshape(4, 4, 2, 8, 128).astype(BF)
            for e in range(2):
                rs_part[e, pl.ds(i * 4, 4), :, n] = part[:, :, e]
        second = mm(low_t[...], hidden[:, pl.ds(at, 256)])
        for e in range(2):
            part = second[:, 128 * e : 128 * e + 128].reshape(16, 2, 8, 128).astype(BF)
            rs_part[e, :, i, 2] = part[:, 0]
            rs_part[e, :, i, 3] = part[:, 1]
        return carry

    lax.fori_loop(0, 4, weights, 0)
    small = [
        mm(sg_t[:, :1024], raw_mid[...]).reshape(16, 2, 8, 128).astype(BF),
        mm(sg_t[:, 1024:], raw_cold[...]).reshape(16, 2, 8, 128).astype(BF),
    ]
    for n in range(8):
        rs_part[n % 2, :, n // 2, 4] = small[(n // 2) % 2][:, n % 2]
    ship(rs_part.at[1 - c], rs_pair, wp_s, wp_r, mate, r).start()
    ship(rs_part.at[1 - c], rs_pair, wp_s, wp_r, mate, r).wait()

    def add_pair(k, carry):
        rs_send[k] = (rs_part[c, k].astype(F32) + rs_pair[k].astype(F32)).astype(BF)
        return carry

    lax.fori_loop(0, 16, add_pair, 0)
    src = r * 4 + y

    def send_block(pg, pr):
        ship(rs_send.at[pr, pg // 2], rs_got.at[src], w_s, w_r, pg, pr).start()

    all_peers(send_block, 2)
    rs_got[src] = rs_send[r, y]
    ship(back_send.at[pl.ds(0, 127)], back_ref.at[pl.ds(0, 127)], b_s, b_r, g, r).wait_recv()
    ph_acc[...] = jnp.zeros_like(ph_acc)

    def hot_weights(i, carry):
        slab = pl.ds(i * 32, 32)
        left = back_ref[slab, 0].astype(F32).reshape(256, 128).T.astype(BF)
        right = back_ref[slab, 1].astype(F32).reshape(256, 128).T.astype(BF)
        own = rows_hot[pl.ds(pl.multiple_of(i * 256, 256), 256), :]
        ph_acc[0:128, :] += mm(left, own)
        ph_acc[128:256, :] += mm(right, own)
        return carry

    lax.fori_loop(0, 4, hot_weights, 0)
    for n in range(4):
        part = ph_acc[:, 128 * n : 128 * n + 128].reshape(16, 2, 8, 128).astype(BF)
        ph_send[:, 2 * n] = part[:, 0]
        ph_send[:, 2 * n + 1] = part[:, 1]

    def send_hot(pg, pr):
        ship(ph_send.at[pr, pg], ph_got.at[me], h_s, h_r, pg, pr).start()

    all_peers(send_hot)
    ph_got[me] = ph_send[r, g]

    ship(q_sum.at[pl.ds(0, 3)], q_recv, qy_s, qy_r, g, r).wait_recv()
    qg = q_sum[3].astype(F32)
    for n in range(3):
        qg += q_recv[n].astype(F32)
    qg_out[...] = qg

    ship(rs_got.at[pl.ds(0, 63)], rs_got.at[pl.ds(0, 63)], w_s, w_r, g, r).wait_recv()

    def add(k, total):
        return total + rs_got[k].astype(F32)

    fin[g, pl.ds(0, 5)] = lax.fori_loop(0, 64, add, jnp.zeros((5, 8, 128), F32))
    ship(ph_got.at[pl.ds(0, 127)], ph_got.at[pl.ds(0, 127)], h_s, h_r, g, r).wait_recv()

    def add_hot(k, total):
        return total + ph_got[k].astype(F32)

    fin[g, 5] = lax.fori_loop(0, 128, add_hot, jnp.zeros((8, 128), F32))
    for k in range(1, 8):
        ship(fin.at[g], fin.at[g], a_s, a_r, (g + k) % 8, r).start()
    ship(fin.at[pl.ds(0, 7)], fin.at[pl.ds(0, 7)], a_s, a_r, g, r).wait()
    fin_ref[...] = fin[...]

    ship(send.at[pl.ds(0, 127)], got.at[pl.ds(0, 127)], f_s, f_r, g, r).wait_send()
    ship(q_all.at[pl.ds(0, 7)], q_all.at[pl.ds(0, 7)], q_s, q_r.at[0], g, r).wait_send()
    ship(lab_all.at[pl.ds(0, 7)], lab_all.at[pl.ds(0, 7)], l_s, l_r, g, r).wait_send()
    for b in range(8):
        ship(stat.at[b, pl.ds(0, 7)], stat.at[b, pl.ds(0, 7)], st_s, st_r.at[0], g, r).wait_send()
    ship(q_send, q_part, qp_s, qp_r.at[0], g, r).wait_send()
    ship(q_sum.at[pl.ds(0, 3)], q_recv, qy_s, qy_r, g, r).wait_send()
    ship(back_send.at[pl.ds(0, 127)], back_ref.at[pl.ds(0, 127)], b_s, b_r, g, r).wait_send()
    ship(rs_got.at[pl.ds(0, 63)], rs_got.at[pl.ds(0, 63)], w_s, w_r, g, r).wait_send()
    ship(ph_got.at[pl.ds(0, 127)], ph_got.at[pl.ds(0, 127)], h_s, h_r, g, r).wait_send()


def scatter_kernel(
    back, served, p_hot, fin, qg_t, loss,
    out_hot, out_mid, out_cold, out_qg, out_loss, o_ph, o_pm, o_pc, o_in, o_out,
    b_hot, b_mid, b_cold,
):
    step = pl.program_id(0)

    @pl.when(step == 0)
    def _():
        lane_seg = lax.broadcasted_iota(jnp.int32, (1, 128), 1) // 32
        zero = jnp.zeros((), BF)
        for i in range(8):
            here = pl.ds(i * 128, 128)
            slab = pl.ds(i * 16, 16)
            b_hot[here, :] = (
                mm_nt(flat(back[slab, 0]), p_hot[:, 0:128])
                + mm_nt(flat(back[slab, 1]), p_hot[:, 128:256])
            ).astype(BF)
            i_mid = to_col(served[1:2, here])
            i_cold = to_col(served[2:3, here])
            mid = flat(back[slab, 2])
            cold = jnp.where(i_cold % 4 == lane_seg, flat(back[slab, 3]), zero)
            for n in range(2):
                lanes = slice(128 * n, 128 * n + 128)
                b_mid[here, lanes] = jnp.where(i_mid // 2048 == n, mid, zero)
                b_cold[here, lanes] = jnp.where(i_cold // 8192 == n, cold, zero)
        out_loss[...] = loss[...]
        for n in range(2):
            o_in[128 * n : 128 * n + 128, :] = fin[:, n].reshape(64, 128).T
        for n in range(8):
            o_out[128 * n : 128 * n + 128, :] = fin[n, 2:4].reshape(16, 128).T
        for n in range(4):
            o_ph[128 * n : 128 * n + 128, :] = fin[2 * n : 2 * n + 2, 5].reshape(16, 128).T
        o_pm[...] = fin[0:2, 4].reshape(16, 128).T
        cold_t = fin[2:4, 4].reshape(16, 128).T
        o_pc[...] = cold_t[0:32] + cold_t[32:64] + cold_t[64:96] + cold_t[96:128]

    out_qg[...] = qg_t[...].T
    idx = served[...]
    hot = picks(idx[0:1] - step * 256, (256, 1024), 0).astype(BF)
    out_hot[...] = mm(hot, b_hot[...])
    mid = picks(idx[1:2] % 2048 - step * 512, (512, 1024), 0).astype(BF)
    both = mm(mid, b_mid[...])
    out_mid[0] = both[:, :128]
    out_mid[1] = both[:, 128:]
    cold = picks((idx[2:3] // 4) % 2048 - step * 512, (512, 1024), 0).astype(BF)
    both = mm(cold, b_cold[...])
    out_cold[0] = both[:, :128]
    out_cold[1] = both[:, 128:]


def local(
    table_hot,
    table_mid,
    table_cold,
    proj_hot,
    proj_mid,
    proj_cold,
    tower_in,
    tower_out,
    queries,
    labels,
    item_slot,
    item_block,
    serve_rows,
):
    served = serve_rows[0]
    anywhere = pl.BlockSpec(memory_space=pl.ANY)
    vmem = pl.BlockSpec(memory_space=pltpu.VMEM)
    sds = jax.ShapeDtypeStruct
    V = pltpu.VMEM
    back, _, qg_t, loss, fin = pl.pallas_call(
        step_kernel,
        out_shape=[
            sds((128, 4, 8, 128), BF),
            sds((1024, 512), BF),
            sds((256, 512), F32),
            sds((1, 512), F32),
            sds((8, 6, 8, 128), F32),
        ],
        in_specs=[anywhere] * 4 + [vmem] * 2 + [anywhere] * 3 + [vmem] * 4,
        out_specs=[vmem] * 5,
        scratch_shapes=[
            V((1024, 512), BF), V((2048, 256), BF), V((2048, 256), BF), V((512, 256), BF),
            V((256, 1024), BF), V((1024, 256), BF), V((8, 512, 256), BF), V((8, 1, 512), jnp.int32),
            V((128, 4, 8, 128), BF), V((128, 4, 8, 128), BF), V((3072, 1024), BF),
            V((256, 3072), BF), V((1024, 128), BF), V((1024, 128), BF), V((128, 256), BF),
            V((256, 128), BF), V((256, 128), BF), V((256, 1024), BF), V((1024, 1024), F32),
            V((1024, 1024), BF), V((1024, 256), F32), V((1024, 256), BF), V((256, 1024), BF),
            V((8, 8, 2, 512), F32), V((8, 1, 512), F32), V((1024, 256), F32),
            V((4, 256, 512), BF), V((4, 256, 512), BF), V((4, 256, 512), BF),
            V((3, 256, 512), BF), V((1024, 1024), BF), V((1024, 256), BF), V((256, 1024), BF),
            V((256, 2048), BF), V((128, 4, 8, 128), BF), V((2, 16, 4, 5, 8, 128), BF),
            V((16, 4, 5, 8, 128), BF), V((16, 4, 5, 8, 128), BF), V((64, 5, 8, 128), BF),
            V((16, 8, 8, 128), BF), V((128, 8, 128), BF), V((256, 512), F32),
            V((8, 6, 8, 128), F32),
            DMA((9,)), DMA, DMA, DMA, DMA((3,)), DMA, DMA, DMA, DMA((8,)), DMA, DMA((4,)),
            DMA, DMA, DMA, DMA, DMA, DMA, DMA, DMA, DMA, DMA, DMA, DMA,
        ],
        compiler_params=pltpu.CompilerParams(
            collective_id=1, has_side_effects=True, vmem_limit_bytes=63 << 20
        ),
        name="step",
    )(
        table_hot, table_mid, table_cold, proj_hot, proj_mid, proj_cold, tower_in, tower_out,
        queries, labels.reshape(1, 512), served, item_slot[0], item_block[0],
    )
    full = lambda a: pl.BlockSpec(a.shape, lambda i: (0,) * a.ndim)
    outs = [
        sds((1024, 512), F32), sds((2, 2048, 128), F32), sds((2, 2048, 128), F32),
        sds((512, 256), F32), sds((1, 512), F32), sds((512, 16), F32), sds((128, 16), F32),
        sds((32, 16), F32), sds((256, 64), F32), sds((1024, 16), F32),
    ]
    grad_hot, grad_mid, grad_cold, query_grad, query_loss, *rest = pl.pallas_call(
        scatter_kernel,
        grid=(4,),
        in_specs=[
            full(back), full(served), full(proj_hot), full(fin),
            pl.BlockSpec((256, 128), lambda i: (0, i)), full(loss),
        ],
        out_specs=[
            pl.BlockSpec((256, 512), lambda i: (i, 0)),
            pl.BlockSpec((2, 512, 128), lambda i: (0, i, 0)),
            pl.BlockSpec((2, 512, 128), lambda i: (0, i, 0)),
            pl.BlockSpec((128, 256), lambda i: (i, 0)),
        ]
        + [full(o) for o in outs[4:]],
        out_shape=outs,
        scratch_shapes=[V((1024, 512), BF), V((1024, 256), BF), V((1024, 256), BF)],
        compiler_params=pltpu.CompilerParams(
            dimension_semantics=("arbitrary",), vmem_limit_bytes=40 << 20
        ),
        name="scatter",
    )(back, served, proj_hot, fin, qg_t, loss)
    return (
        query_loss[0],
        query_grad,
        grad_hot,
        grad_mid.reshape(4096, 128),
        grad_cold.reshape(4096, 128),
        *rest,
    )


def solution(mesh):
    split = P(BOTH)
    return jax.shard_map(
        local,
        mesh=mesh,
        in_specs=(split,) * 3 + (P(),) * 5 + (split,) * 5,
        out_specs=(split,) * 5 + (P(None, "rep"),) * 5,
        check_vma=False,
    )
```

```python
import functools

import jax
import jax.numpy as jnp
from jax import lax
from jax.experimental import pallas as pl
from jax.experimental.pallas import tpu as pltpu
from jax.sharding import PartitionSpec as P

NORM_EPS = 1e-06
LOGIT_SCALE = 0.2
BF = jnp.bfloat16
F32 = jnp.float32
BOTH = ("group", "rep")
MESH = pl.DeviceIdType.MESH
SCALE2 = LOGIT_SCALE * 1.4426950408889634
LN2 = 0.6931471805599453
DMA = pltpu.SemaphoreType.DMA


def mm(a, b):
    return lax.dot_general(a, b, (((1,), (0,)), ((), ())), preferred_element_type=F32)


def mm_nt(a, b):
    return lax.dot_general(a, b, (((1,), (1,)), ((), ())), preferred_element_type=F32)


def mm_tn(a, b):
    return lax.dot_general(a, b, (((0,), (0,)), ((), ())), preferred_element_type=F32)


def flat(block):
    lead = block.shape[0] * block.shape[1]
    return block.astype(F32).reshape(lead, block.shape[2]).astype(BF)


def tiled(value):
    return value.reshape(value.shape[0] // 8, 8, value.shape[1])


def to_col(row):
    return jnp.broadcast_to(row.astype(F32), (128, row.shape[1])).T[:, 0:1].astype(jnp.int32)


def picks(index, shape, axis):
    return jnp.where(index == lax.broadcasted_iota(jnp.int32, shape, axis), 1.0, 0.0)


def step_kernel(
    t_hot, t_mid, t_cold, p_hot, p_mid, proj_cold, w_in, w_out, queries, labels, served,
    item_slot, item_block,
    back_ref, qg_out, loss_out, fin_ref,
    v_hot, v_mid, v_cold, v_ph, v_in, v_out, q_all, lab_all, send, got, rows_hot,
    raw_hot, use_t, slot_t,
    raw_mid, raw_cold, p_cold, p_mid_t, p_cold_t, pooled_t, pre, hidden, resid, vec, vec_t, stat, loss_all, vg,
    q_send, q_part, q_sum, q_recv, pre_g, pool_g, low_t, sg_t, back_send, rs_part,
    rs_pair, rs_send, rs_got, sm_part, sm_pair, sm_send, sm_got, ph_acc, fin,
    in_sem, f_s, f_r, q_s, q_r, l_s, l_r, st_s, st_r, qp_s, qp_r, qy_s, qy_r, b_s, b_r,
    wp_s, wp_r, w_s, w_r, hp_s, hp_r, h_s, h_r, rw_s, rw_r, a_s, a_r,
):
    g = lax.axis_index("group")
    r = lax.axis_index("rep")
    me = g * 16 + r
    y, c = g // 2, g % 2
    mate = y * 2 + 1 - c

    def all_peers(visit, step=1):
        for k in range(0, 8, step):
            pg = lax.rem(g + k, 8)

            def one(j, carry, pg=pg):
                visit(pg, lax.rem(r + j, 16))
                return carry

            lax.fori_loop(0 if k else 1, 16, one, 0)

    def ship(src, dst, s_sem, r_sem, pg, pr):
        return pltpu.make_async_remote_copy(
            src_ref=src,
            dst_ref=dst,
            send_sem=s_sem,
            recv_sem=r_sem,
            device_id=(pg, pr),
            device_id_type=MESH,
        )

    def loads():
        pairs = (
            (t_hot, v_hot), (p_hot, v_ph),
            (t_mid.at[pl.ds(0, 2048)], v_mid.at[:, pl.ds(0, 128)]),
            (t_mid.at[pl.ds(2048, 2048)], v_mid.at[:, pl.ds(128, 128)]),
            (t_cold.at[pl.ds(0, 2048)], v_cold.at[:, pl.ds(0, 128)]),
            (t_cold.at[pl.ds(2048, 2048)], v_cold.at[:, pl.ds(128, 128)]),
            (queries, q_all.at[g]), (w_in, v_in), (w_out, v_out),
        )
        return [pltpu.make_async_copy(a, b, in_sem.at[n]) for n, (a, b) in enumerate(pairs)]

    for copy in loads():
        copy.start()
    barrier = pltpu.get_barrier_semaphore()

    def greet(pg, pr):
        pl.semaphore_signal(barrier, inc=1, device_id=(pg, pr), device_id_type=MESH)

    all_peers(greet)
    lab_all[g] = labels[...]
    held = loads()
    for n in range(4):
        p_cold[pl.ds(32 * n, 32), :] = proj_cold[...]
    p_mid_t[...] = p_mid[...].astype(F32).T.astype(BF)
    p_cold_t[...] = p_cold[...].astype(F32).T.astype(BF)
    for n in range(6):
        held[n].wait()

    lane_seg = lax.broadcasted_iota(jnp.int32, (1, 128), 1) // 32

    def send_rows(k):
        gg = (g + 1 + k) % 8

        def one(j, carry):
            rd = (r + j) % 16
            to = gg * 16 + rd

            @pl.when(to != me)
            def _():
                ship(send.at[to], got.at[me], f_s, f_r, gg, rd).start()

            return carry

        lax.fori_loop(0, 16, one, 0)

    def halves(index, table):
        both = mm(picks(index % 2048, (128, 2048), 1).astype(BF), table[...])
        return jnp.where(index >= 2048, both[:, 128:], both[:, :128])

    def serve(k, carry):
        gg = (g + 1 + k) % 8
        at = pl.multiple_of(gg * 128, 128)
        here = pl.ds(at, 128)
        i_hot, i_mid, i_cold = [to_col(served[n, :, here]) for n in range(3)]
        hot = mm(picks(i_hot, (128, 1024), 1).astype(BF), v_hot[...])
        rows_hot[pl.ds(gg * 16, 16)] = tiled(hot).astype(BF)
        near = mm(hot.astype(BF), v_ph[...])
        mid = halves(i_mid, v_mid)
        line = halves(i_cold // 4, v_cold)
        line = jnp.where(i_cold % 4 == lane_seg, line, 0.0)
        for n, part in enumerate((near[:, :128], near[:, 128:], mid, line)):
            send[pl.ds(gg * 16, 16), n] = tiled(part).astype(BF)
        return carry

    lax.fori_loop(0, 8, serve, 0)
    pl.semaphore_wait(barrier, 127)
    for k in range(8):
        send_rows(k)
    got[me] = send[me]
    held[6].wait()
    for k in range(1, 4):
        ship(q_all.at[g], q_all.at[g], q_s, q_r.at[0], ((y + k) % 4) * 2 + c, r).start()
    ship(q_all.at[g], q_all.at[g], q_s, q_r.at[1], mate, r).start()
    for k in range(1, 8):
        ship(lab_all.at[g], lab_all.at[g], l_s, l_r, (g + k) % 8, r).start()

    where = item_block[...] * 1024 + item_slot[...]

    def count_slots(i, carry):
        at = pl.multiple_of(i * 256, 256)
        idx = where - at
        total = picks(idx[0:1], (256, 1024), 0)
        for f in range(1, 4):
            total += picks(idx[f : f + 1], (256, 1024), 0)
        use_t[pl.ds(at, 256), :] = total.astype(BF)
        return carry

    lax.fori_loop(0, 12, count_slots, 0)
    ship(q_all.at[pl.ds(0, 3)], q_all.at[pl.ds(0, 3)], q_s, q_r.at[0], g, r).wait_recv()
    for k in range(1, 4):
        from_y = ((y + k) % 4) * 2 + c
        ship(q_all.at[from_y], q_all.at[from_y], q_s, q_r.at[2], mate, r).start()

    def send_raw(pg, pr):
        ship(rows_hot.at[pg * 16 + pr], raw_hot.at[me], rw_s, rw_r, pg, pr).start()

    all_peers(send_raw)
    raw_hot[me] = rows_hot[me]

    ship(send.at[pl.ds(0, 127)], got.at[pl.ds(0, 127)], f_s, f_r, g, r).wait_recv()

    def fill(i, carry):
        at = pl.multiple_of(i * 256, 256)
        slab = pl.ds(i * 32, 32)
        for n in range(2):
            near = got[slab, n].astype(F32).reshape(256, 128).T.astype(BF)
            slot_t[pl.ds(128 * n, 128), pl.ds(at, 256)] = near
        mid = flat(got[slab, 2])
        raw_mid[pl.ds(at, 256), :] = mid
        slot_t[:, pl.ds(1024 + at, 256)] = mm_nt(p_mid_t[...], mid).astype(BF)
        cold = flat(got[slab, 3])
        raw_cold[pl.ds(at, 256), :] = cold
        slot_t[:, pl.ds(2048 + at, 256)] = mm_nt(p_cold_t[...], cold).astype(BF)
        return carry

    lax.fori_loop(0, 4, fill, 0)
    held[7].wait()
    held[8].wait()

    def forward(i, carry):
        at = pl.multiple_of(i * 256, 256)
        here = pl.ds(at, 256)
        turned = mm(slot_t[...], use_t[:, here]).astype(BF)
        pooled_t[:, here] = turned
        low32 = turned.astype(F32).T
        low = low32.astype(BF)
        u = mm(low, v_in[...])
        pre[here, :] = u
        h = (u * (1.0 / (1.0 + jnp.exp(-u)))).astype(BF)
        hidden[here, :] = h
        res = low32 + mm(h, v_out[...])
        resid[here, :] = res
        inv = lax.rsqrt(jnp.mean(res * res, axis=1, keepdims=True) + NORM_EPS)
        v = res * inv
        vec[here, :] = v.astype(BF)
        vec_t[:, here] = v.T.astype(BF)
        return carry

    lax.fori_loop(0, 4, forward, 0)

    ship(q_all.at[g], q_all.at[g], q_s, q_r.at[1], mate, r).wait_recv()
    ship(q_all.at[pl.ds(0, 3)], q_all.at[pl.ds(0, 3)], q_s, q_r.at[2], g, r).wait_recv()
    ship(lab_all.at[pl.ds(0, 7)], lab_all.at[pl.ds(0, 7)], l_s, l_r, g, r).wait_recv()

    def order(t):
        return (t % 4) * 2 + t // 4

    def send_stat(b):
        for k in range(1, 8):
            ship(stat.at[b, g], stat.at[b, g], st_s, st_r.at[b], (g + k) % 8, r).start()

    def label_rows(b):
        return lab_all[b] - g * 1024

    def stats(t, carry):
        b = order(t)
        st = mm_nt(vec[...], q_all[b])
        top = jnp.max(st, axis=0, keepdims=True)
        total = jnp.sum(jnp.exp2(st * SCALE2 - top * SCALE2), axis=0, keepdims=True)
        hit = label_rows(b) == lax.broadcasted_iota(jnp.int32, st.shape, 0)
        stat[b, g, pl.ds(0, 1), :] = top * LOGIT_SCALE + jnp.log(total)
        picked = jnp.sum(jnp.where(hit, st, 0.0), axis=0, keepdims=True)
        stat[b, g, pl.ds(1, 1), :] = picked * LOGIT_SCALE

        @pl.when(t > 0)
        def _():
            send_stat(order(t - 1))

        return carry

    lax.fori_loop(0, 8, stats, 0)
    send_stat(7)
    vg[...] = jnp.zeros_like(vg)

    def grads(b):
        ship(stat.at[b, pl.ds(0, 7)], stat.at[b, pl.ds(0, 7)], st_s, st_r.at[b], g, r).wait_recv()
        lses = [stat[b, n, pl.ds(0, 1), :] for n in range(8)]
        top = functools.reduce(jnp.maximum, lses)
        total = functools.reduce(jnp.add, [jnp.exp(v - top) for v in lses])
        joint = top + jnp.log(total)
        hits = functools.reduce(jnp.add, [stat[b, n, pl.ds(1, 1), :] for n in range(8)])
        loss_all[b] = joint - hits
        st = mm_nt(vec[...], q_all[b])
        hit = label_rows(b) == lax.broadcasted_iota(jnp.int32, st.shape, 0)
        prob = jnp.exp2((st * LOGIT_SCALE - joint) * 1.4426950408889634)
        grad = (prob - jnp.where(hit, 1.0, 0.0)).astype(BF)
        vg[...] += mm(grad, q_all[b])
        return LOGIT_SCALE * mm(vec_t[...], grad)

    def for_mate(i, carry):
        q_send[i] = grads(((y + 1 + i) % 4) * 2 + 1 - c).astype(BF)
        ship(q_send.at[i], q_part.at[i], qp_s, qp_r.at[i], mate, r).start()
        return carry

    lax.fori_loop(0, 4, for_mate, 0)

    def for_self(i, carry):
        at_y = (y + 1 + i) % 4
        mine = grads(at_y * 2 + c)
        ship(q_send.at[i], q_part.at[i], qp_s, qp_r.at[i], mate, r).wait_recv()
        q_sum[i] = (mine + q_part[i].astype(F32)).astype(BF)

        @pl.when(i < 3)
        def _():
            ship(q_sum.at[i], q_recv.at[i], qy_s, qy_r, at_y * 2 + c, r).start()

        return carry

    lax.fori_loop(0, 4, for_self, 0)
    loss_out[...] = loss_all[g]

    def backward(i, carry):
        at = pl.multiple_of(i * 256, 256)
        here = pl.ds(at, 256)
        res = resid[here, :]
        inv = lax.rsqrt(jnp.mean(res * res, axis=1, keepdims=True) + NORM_EPS)
        grad = LOGIT_SCALE * vg[here, :]
        dot_wide = jnp.sum(grad * res, axis=1, keepdims=True)
        wg = inv * grad - (inv * inv * inv / 256.0) * res * dot_wide
        low = wg.astype(BF)
        low_t[:, here] = wg.T.astype(BF)
        u = pre[here, :]
        s = 1.0 / (1.0 + jnp.exp(-u))
        pg = (mm_nt(low, v_out[...]) * (s * (1.0 + u * (1.0 - s)))).astype(BF)
        pre_g[here, :] = pg
        pool_g[here, :] = (mm_nt(pg, v_in[...]) + wg).astype(BF)
        return carry

    lax.fori_loop(0, 4, backward, 0)

    def weights(i, carry):
        at = pl.multiple_of(i * 256, 256)
        first = mm(pooled_t[...], pre_g[:, pl.ds(at, 256)]).T
        for n in range(2):
            part = first[:, 128 * n : 128 * n + 128].reshape(4, 4, 2, 8, 128).astype(BF)
            for e in range(2):
                rs_part[e, pl.ds(i * 4, 4), :, n] = part[:, :, e]
        second = mm(low_t[...], hidden[:, pl.ds(at, 256)])
        for e in range(2):
            part = second[:, 128 * e : 128 * e + 128].reshape(16, 2, 8, 128).astype(BF)
            rs_part[e, :, i, 2] = part[:, 0]
            rs_part[e, :, i, 3] = part[:, 1]
        return carry

    lax.fori_loop(0, 4, weights, 0)

    pair = ship(rs_part.at[1 - c], rs_pair, wp_s, wp_r, mate, r)
    pair.start()

    def send_back(t):
        cc = (t + y) % 4

        def one(j, carry):
            to = cc * 32 + (j + r + 16 * c) % 32

            @pl.when(to != me)
            def _():
                ship(back_send.at[to], back_ref.at[me], b_s, b_r, to // 16, to % 16).start()

            return carry

        lax.fori_loop(0, 32, one, 0)

    def slots(t, carry):
        cc = (t + y) % 4
        at = pl.multiple_of(cc * 256, 256)
        slab = pl.ds(cc * 32, 32)
        hot = mm(use_t[pl.ds(at, 256), :], pool_g[...])
        mid = mm(use_t[pl.ds(1024 + at, 256), :], pool_g[...])
        cold = mm(use_t[pl.ds(2048 + at, 256), :], pool_g[...])
        for n, part in enumerate((hot, mid, cold)):
            sg_t[:, pl.ds(n * 1024 + at, 256)] = part.T.astype(BF)
        b_mid = mm_nt(mid.astype(BF), p_mid[...])
        b_cold = mm_nt(cold.astype(BF), p_cold[...])
        for n, part in enumerate((hot[:, :128], hot[:, 128:], b_mid, b_cold)):
            back_send[slab, n] = tiled(part).astype(BF)

        @pl.when(t > 0)
        def _():
            send_back(t - 1)

        return carry

    lax.fori_loop(0, 4, slots, 0)
    send_back(3)
    back_ref[me] = back_send[me]

    ship(rows_hot.at[pl.ds(0, 127)], raw_hot.at[pl.ds(0, 127)], rw_s, rw_r, g, r).wait_recv()
    ph_acc[...] = jnp.zeros_like(ph_acc)

    def hot_weights(i, carry):
        at = pl.multiple_of(i * 256, 256)
        own = raw_hot[pl.ds(i * 32, 32)].astype(F32).reshape(256, 512).astype(BF)
        ph_acc[...] += mm(sg_t[:, pl.ds(at, 256)], own)
        return carry

    lax.fori_loop(0, 4, hot_weights, 0)
    small = [
        mm(sg_t[:, 1024:2048], raw_mid[...]).reshape(16, 2, 8, 128).astype(BF),
        mm(sg_t[:, 2048:], raw_cold[...]).reshape(16, 2, 8, 128).astype(BF),
    ]
    for n in range(8):
        lanes = slice(128 * (n // 2), 128 * (n // 2) + 128)
        part = ph_acc[:, lanes].reshape(16, 2, 8, 128).astype(BF)
        sm_part[n % 2, :, n // 2, 0] = small[(n // 2) % 2][:, n % 2]
        sm_part[n % 2, :, n // 2, 1] = part[:, n % 2]
    small_pair = ship(sm_part.at[1 - c], sm_pair, hp_s, hp_r, mate, r)
    small_pair.start()
    pair.wait()
    src = r * 4 + y

    def add_pair(k, carry):
        rs_send[k] = (rs_part[c, k].astype(F32) + rs_pair[k].astype(F32)).astype(BF)
        return carry

    lax.fori_loop(0, 16, add_pair, 0)

    def send_block(pg, pr):
        ship(rs_send.at[pr, pg // 2], rs_got.at[src], w_s, w_r, pg, pr).start()

    all_peers(send_block, 2)
    rs_got[src] = rs_send[r, y]
    small_pair.wait()

    def add_small(k, carry):
        sm_send[k] = (sm_part[c, k].astype(F32) + sm_pair[k].astype(F32)).astype(BF)
        return carry

    lax.fori_loop(0, 16, add_small, 0)

    def send_small(pg, pr):
        ship(sm_send.at[pr, pg // 2], sm_got.at[src], h_s, h_r, pg, pr).start()

    all_peers(send_small, 2)
    sm_got[src] = sm_send[r, y]

    ship(q_sum.at[pl.ds(0, 3)], q_recv, qy_s, qy_r, g, r).wait_recv()
    qg = q_sum[3].astype(F32)
    for n in range(3):
        qg += q_recv[n].astype(F32)
    qg_out[...] = qg

    ship(rs_got.at[pl.ds(0, 63)], rs_got.at[pl.ds(0, 63)], w_s, w_r, g, r).wait_recv()

    def add(k, total):
        return total + rs_got[k].astype(F32)

    fin[g, pl.ds(0, 4)] = lax.fori_loop(0, 64, add, jnp.zeros((4, 8, 128), F32))
    ship(sm_got.at[pl.ds(0, 63)], sm_got.at[pl.ds(0, 63)], h_s, h_r, g, r).wait_recv()

    def add_rest(k, total):
        return total + sm_got[k].astype(F32)

    fin[g, pl.ds(4, 2)] = lax.fori_loop(0, 64, add_rest, jnp.zeros((2, 8, 128), F32))
    for k in range(1, 8):
        ship(fin.at[g], fin.at[g], a_s, a_r, (g + k) % 8, r).start()
    ship(fin.at[pl.ds(0, 7)], fin.at[pl.ds(0, 7)], a_s, a_r, g, r).wait()
    fin_ref[...] = fin[...]
    ship(back_send.at[pl.ds(0, 127)], back_ref.at[pl.ds(0, 127)], b_s, b_r, g, r).wait_recv()

    ship(send.at[pl.ds(0, 127)], got.at[pl.ds(0, 127)], f_s, f_r, g, r).wait_send()
    ship(q_all.at[pl.ds(0, 7)], q_all.at[pl.ds(0, 7)], q_s, q_r.at[0], g, r).wait_send()
    ship(lab_all.at[pl.ds(0, 7)], lab_all.at[pl.ds(0, 7)], l_s, l_r, g, r).wait_send()
    for b in range(8):
        ship(stat.at[b, pl.ds(0, 7)], stat.at[b, pl.ds(0, 7)], st_s, st_r.at[0], g, r).wait_send()
    ship(q_send, q_part, qp_s, qp_r.at[0], g, r).wait_send()
    ship(q_sum.at[pl.ds(0, 3)], q_recv, qy_s, qy_r, g, r).wait_send()
    ship(back_send.at[pl.ds(0, 127)], back_ref.at[pl.ds(0, 127)], b_s, b_r, g, r).wait_send()
    ship(rs_got.at[pl.ds(0, 63)], rs_got.at[pl.ds(0, 63)], w_s, w_r, g, r).wait_send()
    ship(sm_got.at[pl.ds(0, 63)], sm_got.at[pl.ds(0, 63)], h_s, h_r, g, r).wait_send()
    ship(rows_hot.at[pl.ds(0, 127)], raw_hot.at[pl.ds(0, 127)], rw_s, rw_r, g, r).wait_send()


def scatter_kernel(
    back, served, p_hot, fin, qg_t, loss,
    out_hot, out_mid, out_cold, out_qg, out_loss, o_ph, o_pm, o_pc, o_in, o_out,
    b_hot, b_mid, b_cold,
):
    step = pl.program_id(0)

    @pl.when(step == 0)
    def _():
        lane_seg = lax.broadcasted_iota(jnp.int32, (1, 128), 1) // 32
        zero = jnp.zeros((), BF)
        for i in range(8):
            here = pl.ds(i * 128, 128)
            slab = pl.ds(i * 16, 16)
            b_hot[here, :] = (
                mm_nt(flat(back[slab, 0]), p_hot[:, 0:128])
                + mm_nt(flat(back[slab, 1]), p_hot[:, 128:256])
            ).astype(BF)
            i_mid = to_col(served[1, :, here])
            i_cold = to_col(served[2, :, here])
            mid = flat(back[slab, 2])
            cold = jnp.where(i_cold % 4 == lane_seg, flat(back[slab, 3]), zero)
            for n in range(2):
                lanes = slice(128 * n, 128 * n + 128)
                b_mid[here, lanes] = jnp.where(i_mid // 2048 == n, mid, zero)
                b_cold[here, lanes] = jnp.where(i_cold // 8192 == n, cold, zero)
        out_loss[...] = loss[...]
        for n in range(2):
            o_in[:, 128 * n : 128 * n + 128] = fin[:, n].reshape(64, 128)
        for n in range(8):
            o_out[:, 128 * n : 128 * n + 128] = fin[n, 2:4].reshape(16, 128)
        for n in range(4):
            o_ph[:, 128 * n : 128 * n + 128] = fin[2 * n : 2 * n + 2, 5].reshape(16, 128)
        o_pm[...] = fin[0:2, 4].reshape(16, 128)
        part = fin[2:4, 4].reshape(16, 128)
        o_pc[...] = part[:, 0:32] + part[:, 32:64] + part[:, 64:96] + part[:, 96:128]

    out_qg[...] = qg_t[...].T
    idx = served[...]
    hot = picks(idx[0] - step * 256, (256, 1024), 0).astype(BF)
    out_hot[...] = mm(hot, b_hot[...])
    mid = picks(idx[1] % 2048 - step * 512, (512, 1024), 0).astype(BF)
    both = mm(mid, b_mid[...])
    out_mid[0] = both[:, :128]
    out_mid[1] = both[:, 128:]
    cold = picks((idx[2] // 4) % 2048 - step * 512, (512, 1024), 0).astype(BF)
    both = mm(cold, b_cold[...])
    out_cold[0] = both[:, :128]
    out_cold[1] = both[:, 128:]


def local(
    table_hot,
    table_mid,
    table_cold,
    proj_hot,
    proj_mid,
    proj_cold,
    tower_in,
    tower_out,
    queries,
    labels,
    item_slot,
    item_block,
    serve_rows,
):
    served = serve_rows.transpose(1, 0, 2)
    anywhere = pl.BlockSpec(memory_space=pl.ANY)
    vmem = pl.BlockSpec(memory_space=pltpu.VMEM)
    sds = jax.ShapeDtypeStruct
    V = pltpu.VMEM
    back, qg_t, loss, fin = pl.pallas_call(
        step_kernel,
        out_shape=[
            sds((128, 4, 8, 128), BF),
            sds((256, 512), F32),
            sds((1, 512), F32),
            sds((8, 6, 8, 128), F32),
        ],
        in_specs=[anywhere] * 4 + [vmem] * 2 + [anywhere] * 3 + [vmem] * 4,
        out_specs=[vmem] * 4,
        scratch_shapes=[
            V((1024, 512), BF), V((2048, 256), BF), V((2048, 256), BF), V((512, 256), BF),
            V((256, 1024), BF), V((1024, 256), BF), V((8, 512, 256), BF), V((8, 1, 512), jnp.int32),
            V((128, 4, 8, 128), BF), V((128, 4, 8, 128), BF), V((128, 8, 512), BF),
            V((128, 8, 512), BF), V((3072, 1024), BF),
            V((256, 3072), BF), V((1024, 128), BF), V((1024, 128), BF), V((128, 256), BF),
            V((256, 128), BF), V((256, 128), BF), V((256, 1024), BF), V((1024, 1024), F32),
            V((1024, 1024), BF), V((1024, 256), F32), V((1024, 256), BF), V((256, 1024), BF),
            V((8, 8, 2, 512), F32), V((8, 1, 512), F32), V((1024, 256), F32),
            V((4, 256, 512), BF), V((4, 256, 512), BF), V((4, 256, 512), BF),
            V((3, 256, 512), BF), V((1024, 1024), BF), V((1024, 256), BF), V((256, 1024), BF),
            V((256, 3072), BF), V((128, 4, 8, 128), BF), V((2, 16, 4, 4, 8, 128), BF),
            V((16, 4, 4, 8, 128), BF), V((16, 4, 4, 8, 128), BF), V((64, 4, 8, 128), BF),
            V((2, 16, 4, 2, 8, 128), BF), V((16, 4, 2, 8, 128), BF), V((16, 4, 2, 8, 128), BF),
            V((64, 2, 8, 128), BF), V((256, 512), F32),
            V((8, 6, 8, 128), F32),
            DMA((9,)), DMA, DMA, DMA, DMA((3,)), DMA, DMA, DMA, DMA((8,)), DMA, DMA((4,)),
            DMA, DMA, DMA, DMA, DMA, DMA, DMA, DMA, DMA, DMA, DMA, DMA, DMA, DMA, DMA, DMA,
        ],
        compiler_params=pltpu.CompilerParams(
            collective_id=1, has_side_effects=True, vmem_limit_bytes=63 << 20
        ),
        name="step",
    )(
        table_hot, table_mid, table_cold, proj_hot, proj_mid, proj_cold, tower_in, tower_out,
        queries, labels.reshape(1, 512), served, item_slot[0], item_block[0],
    )
    full = lambda a: pl.BlockSpec(a.shape, lambda i: (0,) * a.ndim)
    outs = [
        sds((1024, 512), F32), sds((2, 2048, 128), F32), sds((2, 2048, 128), F32),
        sds((512, 256), F32), sds((1, 512), F32), sds((16, 512), F32), sds((16, 128), F32),
        sds((16, 32), F32), sds((64, 256), F32), sds((16, 1024), F32),
    ]
    grad_hot, grad_mid, grad_cold, query_grad, query_loss, *rest = pl.pallas_call(
        scatter_kernel,
        grid=(4,),
        in_specs=[
            full(back), full(served), full(proj_hot), full(fin),
            pl.BlockSpec((256, 128), lambda i: (0, i)), full(loss),
        ],
        out_specs=[
            pl.BlockSpec((256, 512), lambda i: (i, 0)),
            pl.BlockSpec((2, 512, 128), lambda i: (0, i, 0)),
            pl.BlockSpec((2, 512, 128), lambda i: (0, i, 0)),
            pl.BlockSpec((128, 256), lambda i: (i, 0)),
        ]
        + [full(o) for o in outs[4:]],
        out_shape=outs,
        scratch_shapes=[V((1024, 512), BF), V((1024, 256), BF), V((1024, 256), BF)],
        compiler_params=pltpu.CompilerParams(
            dimension_semantics=("arbitrary",), vmem_limit_bytes=63 << 20
        ),
        name="scatter",
    )(back, served, proj_hot, fin, qg_t, loss)
    return (
        query_loss[0],
        query_grad,
        grad_hot,
        grad_mid.reshape(4096, 128),
        grad_cold.reshape(4096, 128),
        *[v.T for v in rest],
    )


def solution(mesh):
    split = P(BOTH)
    return jax.shard_map(
        local,
        mesh=mesh,
        in_specs=(split,) * 3 + (P(),) * 5 + (split,) * 5,
        out_specs=(split,) * 5 + (P(None, "rep"),) * 5,
        check_vma=False,
    )
```

```python
import functools

import jax
import jax.numpy as jnp
from jax import lax
from jax.experimental import pallas as pl
from jax.experimental.pallas import tpu as pltpu
from jax.sharding import PartitionSpec as P

NORM_EPS = 1e-06
LOGIT_SCALE = 0.2
BF = jnp.bfloat16
F32 = jnp.float32
BOTH = ("group", "rep")
MESH = pl.DeviceIdType.MESH
SCALE2 = LOGIT_SCALE * 1.4426950408889634
LN2 = 0.6931471805599453
DMA = pltpu.SemaphoreType.DMA


def mm(a, b):
    return lax.dot_general(a, b, (((1,), (0,)), ((), ())), preferred_element_type=F32)


def mm_nt(a, b):
    return lax.dot_general(a, b, (((1,), (1,)), ((), ())), preferred_element_type=F32)


def mm_tn(a, b):
    return lax.dot_general(a, b, (((0,), (0,)), ((), ())), preferred_element_type=F32)


def flat(block):
    lead = block.shape[0] * block.shape[1]
    return block.astype(F32).reshape(lead, block.shape[2]).astype(BF)


def tiled(value):
    return value.reshape(value.shape[0] // 8, 8, value.shape[1])


def to_col(row):
    return jnp.broadcast_to(row.astype(F32), (128, row.shape[1])).T[:, 0:1].astype(jnp.int32)


def picks(index, shape, axis):
    return jnp.where(index == lax.broadcasted_iota(jnp.int32, shape, axis), 1.0, 0.0)


def step_kernel(
    t_hot, t_mid, t_cold, p_hot, p_mid, proj_cold, w_in, w_out, queries, labels, served,
    item_slot, item_block,
    back_ref, qg_out, loss_out, fin_ref,
    v_hot, v_mid, v_cold, v_ph, v_in, v_out, q_all, lab_all, send, got, rows_hot, use_t, slot_t,
    raw_mid, raw_cold, p_cold, p_mid_t, p_cold_t, pooled_t, pre, hidden, resid, vec, vec_t, stat, loss_all, vg,
    q_send, q_part, q_sum, q_recv, q_half, pre_g, pool_g, low_t, sg_t, back_send, rs_part,
    rs_pair, rs_send, rs_got, sm_part, sm_pair, ph_send, ph_got, ph_acc, fin, shares,
    in_sem, f_s, f_r, q_s, q_r, l_s, l_r, st_s, st_r, qp_s, qp_r, qy_s, qy_r, qh_r, b_s, b_r,
    wp_s, wp_r, w_s, w_r, hp_s, hp_r, h_s, h_r, rw_s, rw_r, a_s, a_r,
):
    g = lax.axis_index("group")
    r = lax.axis_index("rep")
    me = g * 16 + r
    y, c = g // 2, g % 2
    mate = y * 2 + 1 - c

    def all_peers(visit, step=1):
        for k in range(0, 8, step):
            pg = lax.rem(g + k, 8)

            def one(j, carry, pg=pg):
                visit(pg, lax.rem(r + j, 16))
                return carry

            lax.fori_loop(0 if k else 1, 16, one, 0, unroll=4 if k else 5)

    def ship(src, dst, s_sem, r_sem, pg, pr):
        return pltpu.make_async_remote_copy(
            src_ref=src,
            dst_ref=dst,
            send_sem=s_sem,
            recv_sem=r_sem,
            device_id=(pg, pr),
            device_id_type=MESH,
        )

    def loads():
        pairs = (
            (t_hot, v_hot), (p_hot, v_ph),
            (t_mid.at[pl.ds(0, 2048)], v_mid.at[:, pl.ds(0, 128)]),
            (t_mid.at[pl.ds(2048, 2048)], v_mid.at[:, pl.ds(128, 128)]),
            (t_cold.at[pl.ds(0, 2048)], v_cold.at[:, pl.ds(0, 128)]),
            (t_cold.at[pl.ds(2048, 2048)], v_cold.at[:, pl.ds(128, 128)]),
            (queries, q_all.at[g]), (w_in, v_in), (w_out, v_out),
        )
        return [pltpu.make_async_copy(a, b, in_sem.at[n]) for n, (a, b) in enumerate(pairs)]

    for copy in loads():
        copy.start()
    barrier = pltpu.get_barrier_semaphore()

    def greet(pg, pr):
        pl.semaphore_signal(barrier, inc=1, device_id=(pg, pr), device_id_type=MESH)

    all_peers(greet)
    lab_all[g] = labels[...]
    held = loads()
    for n in range(4):
        p_cold[pl.ds(32 * n, 32), :] = proj_cold[...]
    p_mid_t[...] = p_mid[...].astype(F32).T.astype(BF)
    p_cold_t[...] = p_cold[...].astype(F32).T.astype(BF)
    for n in range(6):
        held[n].wait()

    lane_seg = lax.broadcasted_iota(jnp.int32, (1, 128), 1) // 32

    def send_rows(k):
        gg = (g + 1 + k) % 8

        def one(j, carry):
            rd = (r + j) % 16
            to = gg * 16 + rd

            @pl.when(to != me)
            def _():
                ship(send.at[to], got.at[me], f_s, f_r, gg, rd).start()

            return carry

        lax.fori_loop(0, 16, one, 0)

    def halves(index, table):
        both = mm(picks(index % 2048, (128, 2048), 1).astype(BF), table[...])
        return jnp.where(index >= 2048, both[:, 128:], both[:, :128])

    def serve(k, carry):
        gg = (g + 1 + k) % 8
        at = pl.multiple_of(gg * 128, 128)
        here = pl.ds(at, 128)
        i_hot, i_mid, i_cold = [to_col(served[n, :, here]) for n in range(3)]
        hot = mm(picks(i_hot, (128, 1024), 1).astype(BF), v_hot[...])
        hot = hot.astype(BF)
        rows_hot[here, :] = hot
        near = mm(hot, v_ph[...])
        mid = halves(i_mid, v_mid)
        line = halves(i_cold // 4, v_cold)
        line = jnp.where(i_cold % 4 == lane_seg, line, 0.0)
        for n, part in enumerate((near[:, :128], near[:, 128:], mid, line)):
            send[pl.ds(gg * 16, 16), n] = tiled(part).astype(BF)
        return carry

    lax.fori_loop(0, 8, serve, 0)
    pl.semaphore_wait(barrier, 127)
    for k in range(8):
        send_rows(k)
    got[me] = send[me]
    held[6].wait()
    up, down, far = [((y + k) % 4) * 2 + c for k in (1, 3, 2)]
    top_half, low_half = pl.ds(0, 256), pl.ds(256, 256)
    ship(q_all.at[g], q_all.at[g], q_s, q_r.at[0], up, r).start()
    ship(q_all.at[g], q_all.at[g], q_s, q_r.at[3], down, r).start()
    ship(q_all.at[g], q_all.at[g], q_s, q_r.at[1], mate, r).start()
    for k in range(1, 8):
        ship(lab_all.at[g], lab_all.at[g], l_s, l_r, (g + k) % 8, r).start()

    where = item_block[...] * 1024 + item_slot[...]

    def count_slots(i, carry):
        at = pl.multiple_of(i * 256, 256)
        idx = where - at
        total = picks(idx[0:1], (256, 1024), 0)
        for f in range(1, 4):
            total += picks(idx[f : f + 1], (256, 1024), 0)
        use_t[pl.ds(at, 256), :] = total.astype(BF)
        return carry

    lax.fori_loop(0, 12, count_slots, 0)
    ship(send.at[pl.ds(0, 127)], got.at[pl.ds(0, 127)], f_s, f_r, g, r).wait_recv()

    def fill(i, carry):
        at = pl.multiple_of(i * 256, 256)
        slab = pl.ds(i * 32, 32)
        for n in range(2):
            near = got[slab, n].astype(F32).reshape(256, 128).T.astype(BF)
            slot_t[pl.ds(128 * n, 128), pl.ds(at, 256)] = near
        mid = flat(got[slab, 2])
        raw_mid[pl.ds(at, 256), :] = mid
        slot_t[:, pl.ds(1024 + at, 256)] = mm_nt(p_mid_t[...], mid).astype(BF)
        cold = flat(got[slab, 3])
        raw_cold[pl.ds(at, 256), :] = cold
        slot_t[:, pl.ds(2048 + at, 256)] = mm_nt(p_cold_t[...], cold).astype(BF)
        return carry

    lax.fori_loop(0, 4, fill, 0)
    held[7].wait()
    held[8].wait()

    def forward(i, carry):
        at = pl.multiple_of(i * 256, 256)
        here = pl.ds(at, 256)
        turned = mm(slot_t[...], use_t[:, here]).astype(BF)
        pooled_t[:, here] = turned
        low32 = turned.astype(F32).T
        low = low32.astype(BF)
        u = mm(low, v_in[...])
        pre[here, :] = u
        h = (u * (1.0 / (1.0 + jnp.exp(-u)))).astype(BF)
        hidden[here, :] = h
        res = low32 + mm(h, v_out[...])
        resid[here, :] = res
        inv = lax.rsqrt(jnp.mean(res * res, axis=1, keepdims=True) + NORM_EPS)
        v = res * inv
        vec[here, :] = v.astype(BF)
        vec_t[:, here] = v.T.astype(BF)
        return carry

    lax.fori_loop(0, 2, forward, 0)

    def onto_mate(block):
        ship(q_all.at[block], q_all.at[block], q_s, q_r.at[2], mate, r).start()

    ship(q_all.at[g], q_all.at[g], q_s, q_r.at[0], up, r).wait_recv()
    ship(q_all.at[down, top_half], q_all.at[down, top_half], q_s, q_r.at[4], up, r).start()
    onto_mate(down)
    ship(q_all.at[g], q_all.at[g], q_s, q_r.at[3], down, r).wait_recv()
    ship(q_all.at[up, low_half], q_all.at[up, low_half], q_s, q_r.at[4], down, r).start()
    onto_mate(up)

    lax.fori_loop(2, 4, forward, 0)
    ship(q_all.at[far], q_all.at[far], q_s, q_r.at[4], up, r).wait_recv()
    onto_mate(far)

    ship(q_all.at[g], q_all.at[g], q_s, q_r.at[1], mate, r).wait_recv()
    ship(q_all.at[pl.ds(0, 3)], q_all.at[pl.ds(0, 3)], q_s, q_r.at[2], g, r).wait_recv()
    ship(lab_all.at[pl.ds(0, 7)], lab_all.at[pl.ds(0, 7)], l_s, l_r, g, r).wait_recv()

    def order(t):
        return (t % 4) * 2 + t // 4

    def send_stat(b):
        for k in range(1, 8):
            ship(stat.at[b, g], stat.at[b, g], st_s, st_r.at[b], (g + k) % 8, r).start()

    def label_rows(b):
        return lab_all[b] - g * 1024

    def stats(t, carry):
        b = order(t)
        st = mm_nt(vec[...], q_all[b])
        top = jnp.max(st, axis=0, keepdims=True)
        total = jnp.sum(jnp.exp2(st * SCALE2 - top * SCALE2), axis=0, keepdims=True)
        hit = label_rows(b) == lax.broadcasted_iota(jnp.int32, st.shape, 0)
        stat[b, g, pl.ds(0, 1), :] = top * LOGIT_SCALE + jnp.log(total)
        picked = jnp.sum(jnp.where(hit, st, 0.0), axis=0, keepdims=True)
        stat[b, g, pl.ds(1, 1), :] = picked * LOGIT_SCALE

        @pl.when(t > 0)
        def _():
            send_stat(order(t - 1))

        return carry

    lax.fori_loop(0, 8, stats, 0)
    send_stat(7)
    vg[...] = jnp.zeros_like(vg)

    def grads(b):
        ship(stat.at[b, pl.ds(0, 7)], stat.at[b, pl.ds(0, 7)], st_s, st_r.at[b], g, r).wait_recv()
        lses = [stat[b, n, pl.ds(0, 1), :] for n in range(8)]
        top = functools.reduce(jnp.maximum, lses)
        total = functools.reduce(jnp.add, [jnp.exp(v - top) for v in lses])
        joint = top + jnp.log(total)
        hits = functools.reduce(jnp.add, [stat[b, n, pl.ds(1, 1), :] for n in range(8)])
        loss_all[b] = joint - hits
        st = mm_nt(vec[...], q_all[b])
        hit = label_rows(b) == lax.broadcasted_iota(jnp.int32, st.shape, 0)
        prob = jnp.exp2((st * LOGIT_SCALE - joint) * 1.4426950408889634)
        grad = (prob - jnp.where(hit, 1.0, 0.0)).astype(BF)
        vg[...] += mm(grad, q_all[b])
        return LOGIT_SCALE * mm(vec_t[...], grad)

    def for_mate(i, carry):
        q_send[i] = grads(((y + 1 + i) % 4) * 2 + 1 - c).astype(BF)
        ship(q_send.at[i], q_part.at[i], qp_s, qp_r.at[i], mate, r).start()
        return carry

    lax.fori_loop(0, 4, for_mate, 0)

    halves_of = (pl.ds(0, 128), pl.ds(128, 128))

    def for_self(t, carry):
        i = t + (1 - 2 * t) * (1 - t // 2)
        mine = grads(((y + 1 + i) % 4) * 2 + c)
        ship(q_send.at[i], q_part.at[i], qp_s, qp_r.at[i], mate, r).wait_recv()
        total = mine + q_part[i].astype(F32)
        q_sum[i] = total.astype(BF)

        @pl.when(t == 0)
        def _():
            for n, to in enumerate((up, down)):
                part = halves_of[n]
                ship(q_sum.at[1, part], q_half.at[n], qy_s, qh_r.at[n], to, r).start()

        for n, to in enumerate((up, down)):

            @pl.when(t == n + 1)
            def _(n=n, to=to):
                part = halves_of[n]
                ship(q_sum.at[1, part], q_half.at[n], qy_s, qh_r.at[n], to, r).wait_recv()
                more = total[128 * n : 128 * n + 128] + q_half[n].astype(F32)
                q_sum[2 * n, part] = more.astype(BF)
                ship(q_sum.at[2 * n], q_recv.at[n], qy_s, qy_r, to, r).start()

        return carry

    lax.fori_loop(0, 4, for_self, 0)
    loss_out[...] = loss_all[g]

    def backward(i, carry):
        at = pl.multiple_of(i * 256, 256)
        here = pl.ds(at, 256)
        res = resid[here, :]
        inv = lax.rsqrt(jnp.mean(res * res, axis=1, keepdims=True) + NORM_EPS)
        grad = LOGIT_SCALE * vg[here, :]
        dot_wide = jnp.sum(grad * res, axis=1, keepdims=True)
        wg = inv * grad - (inv * inv * inv / 256.0) * res * dot_wide
        low = wg.astype(BF)
        low_t[:, here] = wg.T.astype(BF)
        u = pre[here, :]
        s = 1.0 / (1.0 + jnp.exp(-u))
        pg = (mm_nt(low, v_out[...]) * (s * (1.0 + u * (1.0 - s)))).astype(BF)
        pre_g[here, :] = pg
        pool_g[here, :] = (mm_nt(pg, v_in[...]) + wg).astype(BF)
        return carry

    lax.fori_loop(0, 4, backward, 0)

    def weights(i, carry):
        at = pl.multiple_of(i * 256, 256)
        first = mm(pooled_t[...], pre_g[:, pl.ds(at, 256)]).T
        for n in range(2):
            part = first[:, 128 * n : 128 * n + 128].reshape(4, 4, 2, 8, 128).astype(BF)
            for e in range(2):
                rs_part[e, pl.ds(i * 4, 4), :, n] = part[:, :, e]
        second = mm(low_t[...], hidden[:, pl.ds(at, 256)])
        for e in range(2):
            part = second[:, 128 * e : 128 * e + 128].reshape(16, 2, 8, 128).astype(BF)
            rs_part[e, :, i, 2] = part[:, 0]
            rs_part[e, :, i, 3] = part[:, 1]
        return carry

    lax.fori_loop(0, 4, weights, 0)

    pair = ship(rs_part.at[1 - c], rs_pair, wp_s, wp_r, mate, r)
    pair.start()

    def send_back(t):
        cc = (t + y) % 4

        def one(j, carry):
            to = cc * 32 + (j + r + 16 * c) % 32

            @pl.when(to != me)
            def _():
                ship(back_send.at[to], back_ref.at[me], b_s, b_r, to // 16, to % 16).start()

            return carry

        lax.fori_loop(0, 32, one, 0)

    def slots(t, carry):
        cc = (t + y) % 4
        at = pl.multiple_of(cc * 256, 256)
        slab = pl.ds(cc * 32, 32)
        hot = mm(use_t[pl.ds(at, 256), :], pool_g[...])
        mid = mm(use_t[pl.ds(1024 + at, 256), :], pool_g[...])
        cold = mm(use_t[pl.ds(2048 + at, 256), :], pool_g[...])
        for n, part in enumerate((mid, cold)):
            sg_t[:, pl.ds(n * 1024 + at, 256)] = part.T.astype(BF)
        b_mid = mm_nt(mid.astype(BF), p_mid[...])
        b_cold = mm_nt(cold.astype(BF), p_cold[...])
        for n, part in enumerate((hot[:, :128], hot[:, 128:], b_mid, b_cold)):
            back_send[slab, n] = tiled(part).astype(BF)

        @pl.when(t > 0)
        def _():
            send_back(t - 1)

        return carry

    lax.fori_loop(0, 4, slots, 0)
    send_back(3)
    back_ref[me] = back_send[me]

    small = [
        mm(sg_t[:, :1024], raw_mid[...]).reshape(16, 2, 8, 128).astype(BF),
        mm(sg_t[:, 1024:], raw_cold[...]).reshape(16, 2, 8, 128).astype(BF),
    ]
    for n in range(8):
        sm_part[n % 2, :, n // 2] = small[(n // 2) % 2][:, n % 2]
    small_pair = ship(sm_part.at[1 - c], sm_pair, hp_s, hp_r, mate, r)
    small_pair.start()
    pair.wait()
    src = r * 4 + y

    def add_pair(k, carry):
        total = rs_part[c, k].astype(F32) + rs_pair[k].astype(F32)
        rs_send[k, :, pl.ds(0, 4)] = total.astype(BF)
        return carry

    lax.fori_loop(0, 16, add_pair, 0)
    small_pair.wait()

    def add_small(k, carry):
        rs_send[k, :, 4] = (sm_part[c, k].astype(F32) + sm_pair[k].astype(F32)).astype(BF)
        return carry

    lax.fori_loop(0, 16, add_small, 0)

    def send_block(pg, pr):
        ship(rs_send.at[pr, pg // 2], rs_got.at[src], w_s, w_r, pg, pr).start()

    all_peers(send_block, 2)
    rs_got[src] = rs_send[r, y]

    ship(back_send.at[pl.ds(0, 127)], back_ref.at[pl.ds(0, 127)], b_s, b_r, g, r).wait_recv()
    ph_acc[...] = jnp.zeros_like(ph_acc)

    def hot_weights(i, carry):
        slab = pl.ds(i * 32, 32)
        own = rows_hot[pl.ds(pl.multiple_of(i * 256, 256), 256), :]
        for n in range(2):
            turned = back_ref[slab, n].astype(F32).reshape(256, 128).T.astype(BF)
            ph_acc[pl.ds(128 * n, 128), :] += mm(turned, own)
        return carry

    lax.fori_loop(0, 4, hot_weights, 0)
    for n in range(8):
        lanes = slice(128 * (n // 2), 128 * (n // 2) + 128)
        part = ph_acc[:, lanes].reshape(16, 2, 8, 128).astype(BF)
        ph_send[:, n] = part[:, n % 2]

    def send_hot(j, carry):
        pr = lax.rem(r + j, 16)
        ship(ph_send.at[pr], ph_got.at[r], rw_s, rw_r, g, pr).start()
        return carry

    lax.fori_loop(1, 16, send_hot, 0)
    ph_got[r] = ph_send[r]

    ship(q_sum.at[pl.ds(0, 2)], q_recv, qy_s, qy_r, g, r).wait_recv()
    qg = q_sum[3].astype(F32)
    for n in range(2):
        qg += q_recv[n].astype(F32)
    qg_out[...] = qg

    ship(rs_got.at[pl.ds(0, 63)], rs_got.at[pl.ds(0, 63)], w_s, w_r, g, r).wait_recv()

    def add(k, total):
        return total + rs_got[k].astype(F32)

    fin[g] = lax.fori_loop(0, 64, add, jnp.zeros((5, 8, 128), F32))
    for k in range(1, 8):
        ship(fin.at[g], fin.at[g], a_s, a_r, (g + k) % 8, r).start()
    ship(ph_got.at[pl.ds(0, 15)], ph_got.at[pl.ds(0, 15)], rw_s, rw_r, g, r).wait_recv()

    def add_hot(k, total):
        return total + ph_got[k].astype(F32)

    shares[g] = lax.fori_loop(0, 16, add_hot, jnp.zeros((8, 8, 128), F32)).astype(BF)
    for k in range(1, 8):
        ship(shares.at[g], shares.at[g], h_s, h_r, (g + k) % 8, r).start()
    ship(fin.at[pl.ds(0, 7)], fin.at[pl.ds(0, 7)], a_s, a_r, g, r).wait()
    ship(shares.at[pl.ds(0, 7)], shares.at[pl.ds(0, 7)], h_s, h_r, g, r).wait()
    for n in range(8):
        fin_ref[n, pl.ds(0, 5)] = fin[n]
        parts = [shares[k, n].astype(F32) for k in range(8)]
        fin_ref[n, 5] = functools.reduce(jnp.add, parts)

    ship(send.at[pl.ds(0, 127)], got.at[pl.ds(0, 127)], f_s, f_r, g, r).wait_send()
    ship(q_all.at[pl.ds(0, 7)], q_all.at[pl.ds(0, 7)], q_s, q_r.at[0], g, r).wait_send()
    ship(lab_all.at[pl.ds(0, 7)], lab_all.at[pl.ds(0, 7)], l_s, l_r, g, r).wait_send()
    for b in range(8):
        ship(stat.at[b, pl.ds(0, 7)], stat.at[b, pl.ds(0, 7)], st_s, st_r.at[0], g, r).wait_send()
    ship(q_send, q_part, qp_s, qp_r.at[0], g, r).wait_send()
    ship(q_sum.at[pl.ds(0, 3)], q_sum.at[pl.ds(0, 3)], qy_s, qy_r, g, r).wait_send()
    ship(back_send.at[pl.ds(0, 127)], back_ref.at[pl.ds(0, 127)], b_s, b_r, g, r).wait_send()
    ship(rs_got.at[pl.ds(0, 63)], rs_got.at[pl.ds(0, 63)], w_s, w_r, g, r).wait_send()
    ship(ph_got.at[pl.ds(0, 15)], ph_got.at[pl.ds(0, 15)], rw_s, rw_r, g, r).wait_send()


def scatter_kernel(
    back, served, p_hot, fin, qg_t, loss,
    out_hot, out_mid, out_cold, out_qg, out_loss, o_ph, o_pm, o_pc, o_in, o_out,
    b_hot, b_mid, b_cold,
):
    step = pl.program_id(0)

    @pl.when(step == 0)
    def _():
        lane_seg = lax.broadcasted_iota(jnp.int32, (1, 128), 1) // 32
        zero = jnp.zeros((), BF)
        for i in range(8):
            here = pl.ds(i * 128, 128)
            slab = pl.ds(i * 16, 16)
            b_hot[here, :] = (
                mm_nt(flat(back[slab, 0]), p_hot[:, 0:128])
                + mm_nt(flat(back[slab, 1]), p_hot[:, 128:256])
            ).astype(BF)
            i_mid = to_col(served[1, :, here])
            i_cold = to_col(served[2, :, here])
            mid = flat(back[slab, 2])
            cold = jnp.where(i_cold % 4 == lane_seg, flat(back[slab, 3]), zero)
            for n in range(2):
                lanes = slice(128 * n, 128 * n + 128)
                b_mid[here, lanes] = jnp.where(i_mid // 2048 == n, mid, zero)
                b_cold[here, lanes] = jnp.where(i_cold // 8192 == n, cold, zero)
        out_loss[...] = loss[...]
        for n in range(2):
            o_in[:, 128 * n : 128 * n + 128] = fin[:, n].reshape(64, 128)
        for n in range(8):
            o_out[:, 128 * n : 128 * n + 128] = fin[n, 2:4].reshape(16, 128)
        for n in range(4):
            o_ph[:, 128 * n : 128 * n + 128] = fin[2 * n : 2 * n + 2, 5].reshape(16, 128)
        o_pm[...] = fin[0:2, 4].reshape(16, 128)
        part = fin[2:4, 4].reshape(16, 128)
        o_pc[...] = part[:, 0:32] + part[:, 32:64] + part[:, 64:96] + part[:, 96:128]

    out_qg[...] = qg_t[...].T
    idx = served[...]
    hot = picks(idx[0] - step * 256, (256, 1024), 0).astype(BF)
    out_hot[...] = mm(hot, b_hot[...])
    mid = picks(idx[1] % 2048 - step * 512, (512, 1024), 0).astype(BF)
    both = mm(mid, b_mid[...])
    out_mid[0] = both[:, :128]
    out_mid[1] = both[:, 128:]
    cold = picks((idx[2] // 4) % 2048 - step * 512, (512, 1024), 0).astype(BF)
    both = mm(cold, b_cold[...])
    out_cold[0] = both[:, :128]
    out_cold[1] = both[:, 128:]


def local(
    table_hot,
    table_mid,
    table_cold,
    proj_hot,
    proj_mid,
    proj_cold,
    tower_in,
    tower_out,
    queries,
    labels,
    item_slot,
    item_block,
    serve_rows,
):
    served = serve_rows.transpose(1, 0, 2)
    anywhere = pl.BlockSpec(memory_space=pl.ANY)
    vmem = pl.BlockSpec(memory_space=pltpu.VMEM)
    sds = jax.ShapeDtypeStruct
    V = pltpu.VMEM
    back, qg_t, loss, fin = pl.pallas_call(
        step_kernel,
        out_shape=[
            sds((128, 4, 8, 128), BF),
            sds((256, 512), F32),
            sds((1, 512), F32),
            sds((8, 6, 8, 128), F32),
        ],
        in_specs=[anywhere] * 4 + [vmem] * 2 + [anywhere] * 3 + [vmem] * 4,
        out_specs=[vmem] * 4,
        scratch_shapes=[
            V((1024, 512), BF), V((2048, 256), BF), V((2048, 256), BF), V((512, 256), BF),
            V((256, 1024), BF), V((1024, 256), BF), V((8, 512, 256), BF), V((8, 1, 512), jnp.int32),
            V((128, 4, 8, 128), BF), V((128, 4, 8, 128), BF), V((1024, 512), BF),
            V((3072, 1024), BF),
            V((256, 3072), BF), V((1024, 128), BF), V((1024, 128), BF), V((128, 256), BF),
            V((256, 128), BF), V((256, 128), BF), V((256, 1024), BF), V((1024, 1024), F32),
            V((1024, 1024), BF), V((1024, 256), F32), V((1024, 256), BF), V((256, 1024), BF),
            V((8, 8, 2, 512), F32), V((8, 1, 512), F32), V((1024, 256), F32),
            V((4, 256, 512), BF), V((4, 256, 512), BF), V((4, 256, 512), BF),
            V((2, 256, 512), BF), V((2, 128, 512), BF), V((1024, 1024), BF), V((1024, 256), BF), V((256, 1024), BF),
            V((256, 2048), BF), V((128, 4, 8, 128), BF), V((2, 16, 4, 4, 8, 128), BF),
            V((16, 4, 4, 8, 128), BF), V((16, 4, 5, 8, 128), BF), V((64, 5, 8, 128), BF),
            V((2, 16, 4, 8, 128), BF), V((16, 4, 8, 128), BF), V((16, 8, 8, 128), BF),
            V((16, 8, 8, 128), BF), V((256, 512), F32), V((8, 5, 8, 128), F32),
            V((8, 8, 8, 128), BF),
            DMA((9,)), DMA, DMA, DMA, DMA((5,)), DMA, DMA, DMA, DMA((8,)), DMA, DMA((4,)),
            DMA, DMA, DMA((2,)), DMA, DMA, DMA, DMA, DMA, DMA, DMA, DMA, DMA, DMA, DMA, DMA, DMA, DMA,
        ],
        compiler_params=pltpu.CompilerParams(
            collective_id=1, has_side_effects=True, vmem_limit_bytes=63 << 20
        ),
        name="step",
    )(
        table_hot, table_mid, table_cold, proj_hot, proj_mid, proj_cold, tower_in, tower_out,
        queries, labels.reshape(1, 512), served, item_slot[0], item_block[0],
    )
    full = lambda a: pl.BlockSpec(a.shape, lambda i: (0,) * a.ndim)
    outs = [
        sds((1024, 512), F32), sds((2, 2048, 128), F32), sds((2, 2048, 128), F32),
        sds((512, 256), F32), sds((1, 512), F32), sds((16, 512), F32), sds((16, 128), F32),
        sds((16, 32), F32), sds((64, 256), F32), sds((16, 1024), F32),
    ]
    grad_hot, grad_mid, grad_cold, query_grad, query_loss, *rest = pl.pallas_call(
        scatter_kernel,
        grid=(4,),
        in_specs=[
            full(back), full(served), full(proj_hot), full(fin),
            pl.BlockSpec((256, 128), lambda i: (0, i)), full(loss),
        ],
        out_specs=[
            pl.BlockSpec((256, 512), lambda i: (i, 0)),
            pl.BlockSpec((2, 512, 128), lambda i: (0, i, 0)),
            pl.BlockSpec((2, 512, 128), lambda i: (0, i, 0)),
            pl.BlockSpec((128, 256), lambda i: (i, 0)),
        ]
        + [full(o) for o in outs[4:]],
        out_shape=outs,
        scratch_shapes=[V((1024, 512), BF), V((1024, 256), BF), V((1024, 256), BF)],
        compiler_params=pltpu.CompilerParams(
            dimension_semantics=("arbitrary",), vmem_limit_bytes=63 << 20
        ),
        name="scatter",
    )(back, served, proj_hot, fin, qg_t, loss)
    return (
        query_loss[0],
        query_grad,
        grad_hot,
        grad_mid.reshape(4096, 128),
        grad_cold.reshape(4096, 128),
        *[v.T for v in rest],
    )


def solution(mesh):
    split = P(BOTH)
    return jax.shard_map(
        local,
        mesh=mesh,
        in_specs=(split,) * 3 + (P(),) * 5 + (split,) * 5,
        out_specs=(split,) * 5 + (P(None, "rep"),) * 5,
        check_vma=False,
    )
```

```python
import functools

import jax
import jax.numpy as jnp
from jax import lax
from jax.experimental import pallas as pl
from jax.experimental.pallas import tpu as pltpu
from jax.sharding import PartitionSpec as P

NORM_EPS = 1e-06
LOGIT_SCALE = 0.2
BF = jnp.bfloat16
F32 = jnp.float32
BOTH = ("group", "rep")
MESH = pl.DeviceIdType.MESH
LOG2E = 1.4426950408889634
SCALE2 = LOGIT_SCALE * LOG2E
DMA = pltpu.SemaphoreType.DMA


def mm(a, b):
    return lax.dot_general(a, b, (((1,), (0,)), ((), ())), preferred_element_type=F32)


def mm_nt(a, b):
    return lax.dot_general(a, b, (((1,), (1,)), ((), ())), preferred_element_type=F32)


def mm_tn(a, b):
    return lax.dot_general(a, b, (((0,), (0,)), ((), ())), preferred_element_type=F32)


def flat(block):
    lead = block.shape[0] * block.shape[1]
    return block.astype(F32).reshape(lead, block.shape[2]).astype(BF)


def tiled(value):
    return value.reshape(value.shape[0] // 8, 8, value.shape[1])


def to_col(row):
    return jnp.broadcast_to(row.astype(F32), (128, row.shape[1])).T[:, 0:1].astype(jnp.int32)


def picks(index, shape, axis):
    return jnp.where(index == lax.broadcasted_iota(jnp.int32, shape, axis), 1.0, 0.0)


def step_kernel(
    t_hot, t_mid, t_cold, p_hot, p_mid, proj_cold, w_in, w_out, queries, labels, served,
    item_slot, item_block,
    back_ref, qg_out, loss_out, fin_ref,
    v_hot, v_mid, v_cold, v_ph, v_in, v_out, q_all, lab_all, send, got, rows_hot, use_t, slot_t,
    raw_mid, raw_cold, p_cold, p_mid_t, p_cold_t, pooled_t, pre, hidden, resid, vec, vec_t, stat, loss_all, vg,
    q_send, q_part, q_sum, q_recv, q_half, pre_g, pool_g, low_t, sg_t, back_send, rs_part,
    rs_pair, rs_send, rs_got, sm_part, sm_pair, ph_send, ph_got, ph_acc, fin, shares,
    in_sem, f_s, f_r, q_s, q_r, l_s, l_r, st_s, st_r, qp_s, qp_r, qy_s, qy_r, qh_r, b_s, b_r,
    wp_s, wp_r, w_s, w_r, hp_s, hp_r, h_s, h_r, rw_s, rw_r, a_s, a_r,
):
    g = lax.axis_index("group")
    r = lax.axis_index("rep")
    me = g * 16 + r
    y, c = g // 2, g % 2
    mate = y * 2 + 1 - c

    def all_peers(visit, step=1):
        for k in range(0, 8, step):
            pg = lax.rem(g + k, 8)

            def one(j, carry, pg=pg):
                visit(pg, lax.rem(r + j, 16))
                return carry

            lax.fori_loop(0 if k else 1, 16, one, 0, unroll=4 if k else 5)

    def ship(src, dst, s_sem, r_sem, pg, pr):
        return pltpu.make_async_remote_copy(
            src_ref=src,
            dst_ref=dst,
            send_sem=s_sem,
            recv_sem=r_sem,
            device_id=(pg, pr),
            device_id_type=MESH,
        )

    def loads():
        pairs = (
            (t_hot, v_hot), (p_hot, v_ph),
            (t_mid.at[pl.ds(0, 2048)], v_mid.at[:, pl.ds(0, 128)]),
            (t_mid.at[pl.ds(2048, 2048)], v_mid.at[:, pl.ds(128, 128)]),
            (t_cold.at[pl.ds(0, 2048)], v_cold.at[:, pl.ds(0, 128)]),
            (t_cold.at[pl.ds(2048, 2048)], v_cold.at[:, pl.ds(128, 128)]),
            (queries, q_all.at[g]), (w_in, v_in), (w_out, v_out),
        )
        return [pltpu.make_async_copy(a, b, in_sem.at[n]) for n, (a, b) in enumerate(pairs)]

    for copy in loads():
        copy.start()
    barrier = pltpu.get_barrier_semaphore()

    def greet(pg, pr):
        pl.semaphore_signal(barrier, inc=1, device_id=(pg, pr), device_id_type=MESH)

    all_peers(greet)
    lab_all[g] = labels[...]
    held = loads()
    for n in range(4):
        p_cold[pl.ds(32 * n, 32), :] = proj_cold[...]
    p_mid_t[...] = p_mid[...].astype(F32).T.astype(BF)
    p_cold_t[...] = p_cold[...].astype(F32).T.astype(BF)
    for n in range(6):
        held[n].wait()

    lane_seg = lax.broadcasted_iota(jnp.int32, (1, 128), 1) // 32

    def send_rows(k):
        gg = (g + 1 + k) % 8

        def one(j, carry):
            rd = (r + j) % 16
            to = gg * 16 + rd

            @pl.when(to != me)
            def _():
                ship(send.at[to], got.at[me], f_s, f_r, gg, rd).start()

            return carry

        lax.fori_loop(0, 16, one, 0)

    def halves(index, table):
        both = mm(picks(index % 2048, (128, 2048), 1).astype(BF), table[...])
        return jnp.where(index >= 2048, both[:, 128:], both[:, :128])

    def serve(k, carry):
        gg = (g + 1 + k) % 8
        at = pl.multiple_of(gg * 128, 128)
        here = pl.ds(at, 128)
        i_hot, i_mid, i_cold = [to_col(served[n, :, here]) for n in range(3)]
        hot = mm(picks(i_hot, (128, 1024), 1).astype(BF), v_hot[...])
        hot = hot.astype(BF)
        rows_hot[here, :] = hot
        near = mm(hot, v_ph[...])
        mid = halves(i_mid, v_mid)
        line = halves(i_cold // 4, v_cold)
        line = jnp.where(i_cold % 4 == lane_seg, line, 0.0)
        for n, part in enumerate((near[:, :128], near[:, 128:], mid, line)):
            send[pl.ds(gg * 16, 16), n] = tiled(part).astype(BF)
        return carry

    lax.fori_loop(0, 8, serve, 0)
    pl.semaphore_wait(barrier, 127)
    for k in range(8):
        send_rows(k)
    got[me] = send[me]
    held[6].wait()
    up, down, far = [((y + k) % 4) * 2 + c for k in (1, 3, 2)]
    top_half, low_half = pl.ds(0, 256), pl.ds(256, 256)
    ship(q_all.at[g], q_all.at[g], q_s, q_r.at[0], up, r).start()
    ship(q_all.at[g], q_all.at[g], q_s, q_r.at[3], down, r).start()
    ship(q_all.at[g], q_all.at[g], q_s, q_r.at[1], mate, r).start()
    for k in range(1, 8):
        ship(lab_all.at[g], lab_all.at[g], l_s, l_r, (g + k) % 8, r).start()

    where = item_block[...] * 1024 + item_slot[...]

    def count_slots(i, carry):
        at = pl.multiple_of(i * 256, 256)
        idx = where - at
        total = picks(idx[0:1], (256, 1024), 0)
        for f in range(1, 4):
            total += picks(idx[f : f + 1], (256, 1024), 0)
        use_t[pl.ds(at, 256), :] = total.astype(BF)
        return carry

    lax.fori_loop(0, 12, count_slots, 0)
    ship(send.at[pl.ds(0, 127)], got.at[pl.ds(0, 127)], f_s, f_r, g, r).wait_recv()

    def fill(i, carry):
        at = pl.multiple_of(i * 256, 256)
        slab = pl.ds(i * 32, 32)
        for n in range(2):
            near = got[slab, n].astype(F32).reshape(256, 128).T.astype(BF)
            slot_t[pl.ds(128 * n, 128), pl.ds(at, 256)] = near
        mid = flat(got[slab, 2])
        raw_mid[pl.ds(at, 256), :] = mid
        slot_t[:, pl.ds(1024 + at, 256)] = mm_nt(p_mid_t[...], mid).astype(BF)
        cold = flat(got[slab, 3])
        raw_cold[pl.ds(at, 256), :] = cold
        slot_t[:, pl.ds(2048 + at, 256)] = mm_nt(p_cold_t[...], cold).astype(BF)
        return carry

    lax.fori_loop(0, 4, fill, 0)
    held[7].wait()
    held[8].wait()

    def forward(i, carry):
        at = pl.multiple_of(i * 256, 256)
        here = pl.ds(at, 256)
        turned = mm(slot_t[...], use_t[:, here]).astype(BF)
        pooled_t[:, here] = turned
        low32 = turned.astype(F32).T
        low = low32.astype(BF)
        u = mm(low, v_in[...])
        pre[here, :] = u
        h = (u * (1.0 / (1.0 + jnp.exp(-u)))).astype(BF)
        hidden[here, :] = h
        res = low32 + mm(h, v_out[...])
        resid[here, :] = res
        inv = lax.rsqrt(jnp.mean(res * res, axis=1, keepdims=True) + NORM_EPS)
        v = res * inv
        vec[here, :] = v.astype(BF)
        vec_t[:, here] = v.T.astype(BF)
        return carry

    lax.fori_loop(0, 2, forward, 0)

    def onto_mate(block):
        ship(q_all.at[block], q_all.at[block], q_s, q_r.at[2], mate, r).start()

    ship(q_all.at[g], q_all.at[g], q_s, q_r.at[0], up, r).wait_recv()
    ship(q_all.at[down, top_half], q_all.at[down, top_half], q_s, q_r.at[4], up, r).start()
    onto_mate(down)
    ship(q_all.at[g], q_all.at[g], q_s, q_r.at[3], down, r).wait_recv()
    ship(q_all.at[up, low_half], q_all.at[up, low_half], q_s, q_r.at[4], down, r).start()
    onto_mate(up)

    lax.fori_loop(2, 4, forward, 0)
    ship(q_all.at[far], q_all.at[far], q_s, q_r.at[4], up, r).wait_recv()
    onto_mate(far)

    ship(q_all.at[g], q_all.at[g], q_s, q_r.at[1], mate, r).wait_recv()
    ship(q_all.at[pl.ds(0, 3)], q_all.at[pl.ds(0, 3)], q_s, q_r.at[2], g, r).wait_recv()
    ship(lab_all.at[pl.ds(0, 7)], lab_all.at[pl.ds(0, 7)], l_s, l_r, g, r).wait_recv()

    def order(t):
        return (t % 4) * 2 + t // 4

    def send_stat(b):
        for k in range(1, 8):
            ship(stat.at[b, g], stat.at[b, g], st_s, st_r.at[b], (g + k) % 8, r).start()

    def label_rows(b):
        return lab_all[b] - g * 1024

    def stats(t, carry):
        b = order(t)
        st = mm_nt(vec[...], q_all[b])
        top = jnp.max(st, axis=0, keepdims=True)
        total = jnp.sum(jnp.exp2(st * SCALE2 - top * SCALE2), axis=0, keepdims=True)
        hit = label_rows(b) == lax.broadcasted_iota(jnp.int32, st.shape, 0)
        stat[b, g, pl.ds(0, 1), :] = top * LOGIT_SCALE + jnp.log(total)
        picked = jnp.sum(jnp.where(hit, st, 0.0), axis=0, keepdims=True)
        stat[b, g, pl.ds(1, 1), :] = picked * LOGIT_SCALE

        @pl.when(t > 0)
        def _():
            send_stat(order(t - 1))

        return carry

    lax.fori_loop(0, 8, stats, 0)
    send_stat(7)
    vg[...] = jnp.zeros_like(vg)

    def grads(b):
        ship(stat.at[b, pl.ds(0, 7)], stat.at[b, pl.ds(0, 7)], st_s, st_r.at[b], g, r).wait_recv()
        lses = [stat[b, n, pl.ds(0, 1), :] for n in range(8)]
        top = functools.reduce(jnp.maximum, lses)
        total = functools.reduce(jnp.add, [jnp.exp(v - top) for v in lses])
        joint = top + jnp.log(total)
        hits = functools.reduce(jnp.add, [stat[b, n, pl.ds(1, 1), :] for n in range(8)])
        loss_all[b] = joint - hits
        st = mm_nt(vec[...], q_all[b])
        hit = label_rows(b) == lax.broadcasted_iota(jnp.int32, st.shape, 0)
        prob = jnp.exp2(st * SCALE2 - joint * LOG2E)
        grad = (prob - jnp.where(hit, 1.0, 0.0)).astype(BF)
        vg[...] += mm(grad, q_all[b])
        return LOGIT_SCALE * mm(vec_t[...], grad)

    def for_mate(i, carry):
        q_send[i] = grads(((y + 1 + i) % 4) * 2 + 1 - c).astype(BF)
        ship(q_send.at[i], q_part.at[i], qp_s, qp_r.at[i], mate, r).start()
        return carry

    lax.fori_loop(0, 4, for_mate, 0)

    halves_of = (pl.ds(0, 128), pl.ds(128, 128))

    def for_self(t, carry):
        i = t + (1 - 2 * t) * (1 - t // 2)
        mine = grads(((y + 1 + i) % 4) * 2 + c)
        ship(q_send.at[i], q_part.at[i], qp_s, qp_r.at[i], mate, r).wait_recv()
        total = mine + q_part[i].astype(F32)
        q_sum[i] = total.astype(BF)

        @pl.when(t == 0)
        def _():
            for n, to in enumerate((up, down)):
                part = halves_of[n]
                ship(q_sum.at[1, part], q_half.at[n], qy_s, qh_r.at[n], to, r).start()

        for n, to in enumerate((up, down)):

            @pl.when(t == n + 1)
            def _(n=n, to=to):
                part = halves_of[n]
                ship(q_sum.at[1, part], q_half.at[n], qy_s, qh_r.at[n], to, r).wait_recv()
                more = total[128 * n : 128 * n + 128] + q_half[n].astype(F32)
                q_sum[2 * n, part] = more.astype(BF)
                ship(q_sum.at[2 * n], q_recv.at[n], qy_s, qy_r, to, r).start()

        return carry

    lax.fori_loop(0, 4, for_self, 0)
    loss_out[...] = loss_all[g]

    def backward(i, carry):
        at = pl.multiple_of(i * 256, 256)
        here = pl.ds(at, 256)
        res = resid[here, :]
        inv = lax.rsqrt(jnp.mean(res * res, axis=1, keepdims=True) + NORM_EPS)
        grad = LOGIT_SCALE * vg[here, :]
        dot_wide = jnp.sum(grad * res, axis=1, keepdims=True)
        wg = inv * grad - (inv * inv * inv / 256.0) * res * dot_wide
        low = wg.astype(BF)
        low_t[:, here] = wg.T.astype(BF)
        u = pre[here, :]
        s = 1.0 / (1.0 + jnp.exp(-u))
        pg = (mm_nt(low, v_out[...]) * (s * (1.0 + u * (1.0 - s)))).astype(BF)
        pre_g[here, :] = pg
        pool_g[here, :] = (mm_nt(pg, v_in[...]) + wg).astype(BF)
        return carry

    lax.fori_loop(0, 4, backward, 0)

    def weights(i, carry):
        at = pl.multiple_of(i * 256, 256)
        first = mm(pooled_t[...], pre_g[:, pl.ds(at, 256)]).T
        for n in range(2):
            part = first[:, 128 * n : 128 * n + 128].reshape(4, 4, 2, 8, 128).astype(BF)
            for e in range(2):
                rs_part[e, pl.ds(i * 4, 4), :, n] = part[:, :, e]
        second = mm(low_t[...], hidden[:, pl.ds(at, 256)])
        for e in range(2):
            part = second[:, 128 * e : 128 * e + 128].reshape(16, 2, 8, 128).astype(BF)
            rs_part[e, :, i, 2] = part[:, 0]
            rs_part[e, :, i, 3] = part[:, 1]
        return carry

    lax.fori_loop(0, 4, weights, 0)

    pair = ship(rs_part.at[1 - c], rs_pair, wp_s, wp_r, mate, r)
    pair.start()

    def send_back(t):
        cc = (t + y) % 4

        def one(j, carry):
            to = cc * 32 + (j + r + 16 * c) % 32

            @pl.when(to != me)
            def _():
                ship(back_send.at[to], back_ref.at[me], b_s, b_r, to // 16, to % 16).start()

            return carry

        lax.fori_loop(0, 32, one, 0)

    def slots(t, carry):
        cc = (t + y) % 4
        at = pl.multiple_of(cc * 256, 256)
        slab = pl.ds(cc * 32, 32)
        hot = mm(use_t[pl.ds(at, 256), :], pool_g[...])
        mid = mm(use_t[pl.ds(1024 + at, 256), :], pool_g[...])
        cold = mm(use_t[pl.ds(2048 + at, 256), :], pool_g[...])
        for n, part in enumerate((mid, cold)):
            sg_t[:, pl.ds(n * 1024 + at, 256)] = part.T.astype(BF)
        b_mid = mm_nt(mid.astype(BF), p_mid[...])
        b_cold = mm_nt(cold.astype(BF), p_cold[...])
        for n, part in enumerate((hot[:, :128], hot[:, 128:], b_mid, b_cold)):
            back_send[slab, n] = tiled(part).astype(BF)

        @pl.when(t > 0)
        def _():
            send_back(t - 1)

        return carry

    lax.fori_loop(0, 4, slots, 0)
    send_back(3)
    back_ref[me] = back_send[me]

    small = [
        mm(sg_t[:, :1024], raw_mid[...]).reshape(16, 2, 8, 128).astype(BF),
        mm(sg_t[:, 1024:], raw_cold[...]).reshape(16, 2, 8, 128).astype(BF),
    ]
    for n in range(8):
        sm_part[n % 2, :, n // 2] = small[(n // 2) % 2][:, n % 2]
    small_pair = ship(sm_part.at[1 - c], sm_pair, hp_s, hp_r, mate, r)
    small_pair.start()
    pair.wait()
    src = r * 4 + y

    def add_pair(k, carry):
        total = rs_part[c, k].astype(F32) + rs_pair[k].astype(F32)
        rs_send[k, :, pl.ds(0, 4)] = total.astype(BF)
        return carry

    lax.fori_loop(0, 16, add_pair, 0)
    small_pair.wait()

    def add_small(k, carry):
        rs_send[k, :, 4] = (sm_part[c, k].astype(F32) + sm_pair[k].astype(F32)).astype(BF)
        return carry

    lax.fori_loop(0, 16, add_small, 0)

    def send_block(pg, pr):
        ship(rs_send.at[pr, pg // 2], rs_got.at[src], w_s, w_r, pg, pr).start()

    all_peers(send_block, 2)
    rs_got[src] = rs_send[r, y]

    ship(back_send.at[pl.ds(0, 127)], back_ref.at[pl.ds(0, 127)], b_s, b_r, g, r).wait_recv()
    ph_acc[...] = jnp.zeros_like(ph_acc)

    def hot_weights(i, carry):
        slab = pl.ds(i * 32, 32)
        own = rows_hot[pl.ds(pl.multiple_of(i * 256, 256), 256), :]
        for n in range(2):
            turned = back_ref[slab, n].astype(F32).reshape(256, 128).T.astype(BF)
            ph_acc[pl.ds(128 * n, 128), :] += mm(turned, own)
        return carry

    lax.fori_loop(0, 4, hot_weights, 0)
    for n in range(8):
        lanes = slice(128 * (n // 2), 128 * (n // 2) + 128)
        part = ph_acc[:, lanes].reshape(16, 2, 8, 128).astype(BF)
        ph_send[:, n] = part[:, n % 2]

    def send_hot(j, carry):
        pr = lax.rem(r + j, 16)
        ship(ph_send.at[pr], ph_got.at[r], rw_s, rw_r, g, pr).start()
        return carry

    lax.fori_loop(1, 16, send_hot, 0)
    ph_got[r] = ph_send[r]

    ship(q_sum.at[pl.ds(0, 2)], q_recv, qy_s, qy_r, g, r).wait_recv()
    qg = q_sum[3].astype(F32)
    for n in range(2):
        qg += q_recv[n].astype(F32)
    qg_out[...] = qg

    ship(rs_got.at[pl.ds(0, 63)], rs_got.at[pl.ds(0, 63)], w_s, w_r, g, r).wait_recv()

    def add(k, total):
        return total + rs_got[k].astype(F32)

    fin[g] = lax.fori_loop(0, 64, add, jnp.zeros((5, 8, 128), F32))
    for k in range(1, 8):
        ship(fin.at[g], fin.at[g], a_s, a_r, (g + k) % 8, r).start()
    ship(ph_got.at[pl.ds(0, 15)], ph_got.at[pl.ds(0, 15)], rw_s, rw_r, g, r).wait_recv()

    def add_hot(k, total):
        return total + ph_got[k].astype(F32)

    shares[g] = lax.fori_loop(0, 16, add_hot, jnp.zeros((8, 8, 128), F32)).astype(BF)
    for k in range(1, 8):
        ship(shares.at[g], shares.at[g], h_s, h_r, (g + k) % 8, r).start()
    ship(fin.at[pl.ds(0, 7)], fin.at[pl.ds(0, 7)], a_s, a_r, g, r).wait()
    ship(shares.at[pl.ds(0, 7)], shares.at[pl.ds(0, 7)], h_s, h_r, g, r).wait()
    for n in range(8):
        fin_ref[n, pl.ds(0, 5)] = fin[n]
        parts = [shares[k, n].astype(F32) for k in range(8)]
        fin_ref[n, 5] = functools.reduce(jnp.add, parts)

    ship(send.at[pl.ds(0, 127)], got.at[pl.ds(0, 127)], f_s, f_r, g, r).wait_send()
    ship(q_all.at[pl.ds(0, 7)], q_all.at[pl.ds(0, 7)], q_s, q_r.at[0], g, r).wait_send()
    ship(lab_all.at[pl.ds(0, 7)], lab_all.at[pl.ds(0, 7)], l_s, l_r, g, r).wait_send()
    for b in range(8):
        ship(stat.at[b, pl.ds(0, 7)], stat.at[b, pl.ds(0, 7)], st_s, st_r.at[0], g, r).wait_send()
    ship(q_send, q_part, qp_s, qp_r.at[0], g, r).wait_send()
    ship(q_sum.at[pl.ds(0, 3)], q_sum.at[pl.ds(0, 3)], qy_s, qy_r, g, r).wait_send()
    ship(back_send.at[pl.ds(0, 127)], back_ref.at[pl.ds(0, 127)], b_s, b_r, g, r).wait_send()
    ship(rs_got.at[pl.ds(0, 63)], rs_got.at[pl.ds(0, 63)], w_s, w_r, g, r).wait_send()
    ship(ph_got.at[pl.ds(0, 15)], ph_got.at[pl.ds(0, 15)], rw_s, rw_r, g, r).wait_send()


def scatter_kernel(
    back, served, p_hot, fin, qg_t, loss,
    out_hot, out_mid, out_cold, out_qg, out_loss, o_ph, o_pm, o_pc, o_in, o_out,
    b_hot, b_mid, b_cold,
):
    step = pl.program_id(0)

    @pl.when(step == 0)
    def _():
        lane_seg = lax.broadcasted_iota(jnp.int32, (1, 128), 1) // 32
        zero = jnp.zeros((), BF)
        for i in range(8):
            here = pl.ds(i * 128, 128)
            slab = pl.ds(i * 16, 16)
            b_hot[here, :] = (
                mm_nt(flat(back[slab, 0]), p_hot[:, 0:128])
                + mm_nt(flat(back[slab, 1]), p_hot[:, 128:256])
            ).astype(BF)
            i_mid = to_col(served[1, :, here])
            i_cold = to_col(served[2, :, here])
            mid = flat(back[slab, 2])
            cold = jnp.where(i_cold % 4 == lane_seg, flat(back[slab, 3]), zero)
            for n in range(2):
                lanes = slice(128 * n, 128 * n + 128)
                b_mid[here, lanes] = jnp.where(i_mid // 2048 == n, mid, zero)
                b_cold[here, lanes] = jnp.where(i_cold // 8192 == n, cold, zero)
        out_loss[...] = loss[...]
        for n in range(2):
            o_in[:, 128 * n : 128 * n + 128] = fin[:, n].reshape(64, 128)
        for n in range(8):
            o_out[:, 128 * n : 128 * n + 128] = fin[n, 2:4].reshape(16, 128)
        for n in range(4):
            o_ph[:, 128 * n : 128 * n + 128] = fin[2 * n : 2 * n + 2, 5].reshape(16, 128)
        o_pm[...] = fin[0:2, 4].reshape(16, 128)
        part = fin[2:4, 4].reshape(16, 128)
        o_pc[...] = part[:, 0:32] + part[:, 32:64] + part[:, 64:96] + part[:, 96:128]

    out_qg[...] = qg_t[...].T
    idx = served[...]
    hot = picks(idx[0] - step * 256, (256, 1024), 0).astype(BF)
    out_hot[...] = mm(hot, b_hot[...])
    mid = picks(idx[1] % 2048 - step * 512, (512, 1024), 0).astype(BF)
    both = mm(mid, b_mid[...])
    out_mid[0] = both[:, :128]
    out_mid[1] = both[:, 128:]
    cold = picks((idx[2] // 4) % 2048 - step * 512, (512, 1024), 0).astype(BF)
    both = mm(cold, b_cold[...])
    out_cold[0] = both[:, :128]
    out_cold[1] = both[:, 128:]


def local(
    table_hot,
    table_mid,
    table_cold,
    proj_hot,
    proj_mid,
    proj_cold,
    tower_in,
    tower_out,
    queries,
    labels,
    item_slot,
    item_block,
    serve_rows,
):
    served = serve_rows.transpose(1, 0, 2)
    anywhere = pl.BlockSpec(memory_space=pl.ANY)
    vmem = pl.BlockSpec(memory_space=pltpu.VMEM)
    sds = jax.ShapeDtypeStruct
    V = pltpu.VMEM
    back, qg_t, loss, fin = pl.pallas_call(
        step_kernel,
        out_shape=[
            sds((128, 4, 8, 128), BF),
            sds((256, 512), F32),
            sds((1, 512), F32),
            sds((8, 6, 8, 128), F32),
        ],
        in_specs=[anywhere] * 4 + [vmem] * 2 + [anywhere] * 3 + [vmem] * 4,
        out_specs=[vmem] * 4,
        scratch_shapes=[
            V((1024, 512), BF), V((2048, 256), BF), V((2048, 256), BF), V((512, 256), BF),
            V((256, 1024), BF), V((1024, 256), BF), V((8, 512, 256), BF), V((8, 1, 512), jnp.int32),
            V((128, 4, 8, 128), BF), V((128, 4, 8, 128), BF), V((1024, 512), BF),
            V((3072, 1024), BF),
            V((256, 3072), BF), V((1024, 128), BF), V((1024, 128), BF), V((128, 256), BF),
            V((256, 128), BF), V((256, 128), BF), V((256, 1024), BF), V((1024, 1024), F32),
            V((1024, 1024), BF), V((1024, 256), F32), V((1024, 256), BF), V((256, 1024), BF),
            V((8, 8, 2, 512), F32), V((8, 1, 512), F32), V((1024, 256), F32),
            V((4, 256, 512), BF), V((4, 256, 512), BF), V((4, 256, 512), BF),
            V((2, 256, 512), BF), V((2, 128, 512), BF), V((1024, 1024), BF), V((1024, 256), BF), V((256, 1024), BF),
            V((256, 2048), BF), V((128, 4, 8, 128), BF), V((2, 16, 4, 4, 8, 128), BF),
            V((16, 4, 4, 8, 128), BF), V((16, 4, 5, 8, 128), BF), V((64, 5, 8, 128), BF),
            V((2, 16, 4, 8, 128), BF), V((16, 4, 8, 128), BF), V((16, 8, 8, 128), BF),
            V((16, 8, 8, 128), BF), V((256, 512), F32), V((8, 5, 8, 128), F32),
            V((8, 8, 8, 128), BF),
            DMA((9,)), DMA, DMA, DMA, DMA((5,)), DMA, DMA, DMA, DMA((8,)), DMA, DMA((4,)),
            DMA, DMA, DMA((2,)), DMA, DMA, DMA, DMA, DMA, DMA, DMA, DMA, DMA, DMA, DMA, DMA, DMA, DMA,
        ],
        compiler_params=pltpu.CompilerParams(
            collective_id=1, has_side_effects=True, vmem_limit_bytes=63 << 20
        ),
        name="step",
    )(
        table_hot, table_mid, table_cold, proj_hot, proj_mid, proj_cold, tower_in, tower_out,
        queries, labels.reshape(1, 512), served, item_slot[0], item_block[0],
    )
    full = lambda a: pl.BlockSpec(a.shape, lambda i: (0,) * a.ndim)
    outs = [
        sds((1024, 512), F32), sds((2, 2048, 128), F32), sds((2, 2048, 128), F32),
        sds((512, 256), F32), sds((1, 512), F32), sds((16, 512), F32), sds((16, 128), F32),
        sds((16, 32), F32), sds((64, 256), F32), sds((16, 1024), F32),
    ]
    grad_hot, grad_mid, grad_cold, query_grad, query_loss, *rest = pl.pallas_call(
        scatter_kernel,
        grid=(4,),
        in_specs=[
            full(back), full(served), full(proj_hot), full(fin),
            pl.BlockSpec((256, 128), lambda i: (0, i)), full(loss),
        ],
        out_specs=[
            pl.BlockSpec((256, 512), lambda i: (i, 0)),
            pl.BlockSpec((2, 512, 128), lambda i: (0, i, 0)),
            pl.BlockSpec((2, 512, 128), lambda i: (0, i, 0)),
            pl.BlockSpec((128, 256), lambda i: (i, 0)),
        ]
        + [full(o) for o in outs[4:]],
        out_shape=outs,
        scratch_shapes=[V((1024, 512), BF), V((1024, 256), BF), V((1024, 256), BF)],
        compiler_params=pltpu.CompilerParams(
            dimension_semantics=("arbitrary",), vmem_limit_bytes=63 << 20
        ),
        name="scatter",
    )(back, served, proj_hot, fin, qg_t, loss)
    return (
        query_loss[0],
        query_grad,
        grad_hot,
        grad_mid.reshape(4096, 128),
        grad_cold.reshape(4096, 128),
        *[v.T for v in rest],
    )


def solution(mesh):
    split = P(BOTH)
    return jax.shard_map(
        local,
        mesh=mesh,
        in_specs=(split,) * 3 + (P(),) * 5 + (split,) * 5,
        out_specs=(split,) * 5 + (P(None, "rep"),) * 5,
        check_vma=False,
    )
```
